256 devices in a mesh: row: 8 (over x, z_hi), col: 8 (over z_lo, core), depth: 4 (over y).
Axes of the slice: x: 4, y: 4, z: 8 (z_hi: 2, z_lo: 4; z = z_hi * 4 + z_lo), core: 2. Of those that a mesh axis runs over, the one named last changes fastest.
Arguments:
- tokens: bfloat16 [1024, 4096], P(('col', 'depth'), 'row'), may hold values from -72 to 72
- norm_gain: float32 [4096], P('row'), may hold values from 0.25 to 1.75
- w_gate: bfloat16 [4096, 14336], P('row', 'col'), may hold values from -0.09375 to 0.09375
- w_up: bfloat16 [4096, 14336], P('row', 'col'), may hold values from -0.09375 to 0.09375
- w_down: bfloat16 [14336, 4096], P('col', 'row'), may hold values from -0.046875 to 0.046875
- cotangent: bfloat16 [1024, 4096], P(('col', 'depth'), 'row'), may hold values from -1.5 to 1.5
Outputs:
- output: bfloat16 [1024, 4096], P(('col', 'depth'), 'row')
- grad_tokens: bfloat16 [1024, 4096], P(('col', 'depth'), 'row')
- grad_gain: float32 [4096], P('row')
- grad_gate: bfloat16 [4096, 14336], P('row', 'col')
- grad_up: bfloat16 [4096, 14336], P('row', 'col')
- grad_down: bfloat16 [14336, 4096], P('col', 'row')
The draws below stay inside these ranges and needn't reach their ends.
All inputs are finite; a program needn't handle non-finite values.
Results may differ from the reference program's by a relative error of at most 0.023.
Values may be sent and summed in bfloat16 or wider, within the bound.
No kernel may reach another device: no remote copies, remote signals or barrier semaphores. Data moves between devices by JAX's collectives and lax.ppermute only.
A program may use at most 64 MiB of HBM per device.

```python
import jax
import jax.numpy as jnp
from jax import lax

D = 4096
FF = 14336
TOK_DEV = 32
TOKENS = 1024
N_ROW = 8
N_COL = 8
N_DEPTH = 4


def draw_tokens(key, part):
    key_base, key_cols, key_rows = jax.random.split(jax.random.fold_in(key, 7), 3)
    feature = jnp.arange(D, dtype=jnp.float32) / D - 0.5
    position = jnp.arange(TOKENS, dtype=jnp.float32) / TOKENS
    row_scale = 0.5 * jnp.exp(1.1 * position + jax.random.uniform(key_rows, (TOKENS,), jnp.float32, -0.8, 0.8))
    col_scale = jnp.exp(1.7 * feature + jax.random.uniform(key_cols, (D,), jnp.float32, -0.8, 0.8))
    base = jax.random.truncated_normal(key_base, -4.0, 4.0, (TOKENS, D), jnp.float32)
    return (base * row_scale[:, None] * col_scale[None, :]).astype(jnp.bfloat16)


def block_scale(stream_key, shape, cuts, least, top_value):
    loudness, own = 1.0, jax.random.fold_in(stream_key, 6)
    for axis_at, blocks in cuts:
        heights = jnp.exp(jax.random.uniform(jax.random.fold_in(own, axis_at), (blocks,), jnp.float32, least / len(cuts), top_value / len(cuts)))
        loudness = loudness * jnp.repeat(heights, shape[axis_at] // blocks).reshape([-1 if axis == axis_at else 1 for axis in range(len(shape))])
    return loudness


def scatter_about(stream_key, extent, deviation, bound, pieces=(), kind=jnp.bfloat16):
    values = deviation * jax.random.normal(stream_key, extent, jnp.float32)
    if pieces:
        values = values * block_scale(stream_key, extent, pieces, -0.22, 0.18)
    return jnp.clip(values, -bound, bound).astype(kind)


def setup_inputs(seed: int = 0) -> dict:
    arg_keys = jax.random.split(jax.random.key(seed), 7)
    return {
        "tokens": draw_tokens(jax.random.fold_in(arg_keys[6], 71), 0),
        "norm_gain": jnp.clip(1.0 + 0.15 * jax.random.normal(arg_keys[1], (D,), jnp.float32), 0.25, 1.75),
        "w_gate": scatter_about(arg_keys[2], (D, FF), D ** -0.5, 0.09375, ((0, 8), (1, 8))),
        "w_up": scatter_about(arg_keys[3], (D, FF), D ** -0.5, 0.09375, ((0, 8), (1, 8))),
        "w_down": scatter_about(arg_keys[4], (FF, D), FF ** -0.5, 0.046875, ((0, 8), (1, 8))),
        "cotangent": scatter_about(arg_keys[5], (TOKENS, D), 0.25, 1.5, ((0, 32), (1, 8))),
    }


EPS = 1e-05

def rounded(value):
    low = lax.optimization_barrier(value.astype(jnp.bfloat16))
    return low.astype(jnp.float32)

def block_sum(left, right, parts):
    size = left.shape[1] // parts
    total = jnp.zeros((left.shape[0], right.shape[1]), jnp.float32)
    for index in range(parts):
        piece = jnp.dot(left[:, index * size:(index + 1) * size], right[index * size:(index + 1) * size], preferred_element_type=jnp.float32)
        total = total + rounded(piece)
    return total

def group_rows(array, group):
    shaped = array.reshape(N_COL, N_DEPTH, TOK_DEV, array.shape[1])
    return shaped[:, group].reshape(N_COL * TOK_DEV, array.shape[1])

def reference(tokens, norm_gain, w_gate, w_up, w_down, cotangent):
    inputs = tokens.astype(jnp.float32)
    inv_rms = lax.rsqrt(lax.optimization_barrier(jnp.sum(inputs * inputs, axis=1, keepdims=True)) / D + EPS)
    normal_rows = inputs * inv_rms
    normed = (normal_rows * norm_gain[None, :]).astype(jnp.bfloat16)
    gate = block_sum(normed, w_gate, N_ROW)
    up = block_sum(normed, w_up, N_ROW)
    sig = jax.nn.sigmoid(gate)
    act = gate * sig
    hidden = (act * up).astype(jnp.bfloat16)
    mixed = block_sum(hidden, w_down, N_COL)
    output = (inputs + mixed).astype(jnp.bfloat16)
    grad_hidden = block_sum(cotangent, w_down.T, N_ROW)
    grad_up_h = (grad_hidden * act).astype(jnp.bfloat16)
    grad_gate_h = (grad_hidden * up * sig * (1.0 + gate * (1.0 - sig))).astype(jnp.bfloat16)
    size = FF // N_COL
    grad_normed = jnp.zeros((TOKENS, D), jnp.float32)
    for index in range(N_COL):
        cols = slice(index * size, (index + 1) * size)
        piece = jnp.dot(grad_gate_h[:, cols], w_gate[:, cols].T, preferred_element_type=jnp.float32)
        piece = piece + jnp.dot(grad_up_h[:, cols], w_up[:, cols].T, preferred_element_type=jnp.float32)
        grad_normed = grad_normed + rounded(piece)
    grad_scaled = grad_normed * norm_gain[None, :]
    proj = lax.optimization_barrier(jnp.sum(grad_scaled * normal_rows, axis=1, keepdims=True))
    grad_tokens = (cotangent.astype(jnp.float32) + inv_rms * (grad_scaled - normal_rows * proj / D)).astype(jnp.bfloat16)
    grad_gain = lax.optimization_barrier(jnp.sum(grad_normed * normal_rows, axis=0))
    sum_gate = jnp.zeros((D, FF), jnp.float32)
    sum_up = jnp.zeros((D, FF), jnp.float32)
    sum_down = jnp.zeros((FF, D), jnp.float32)
    for group in range(N_DEPTH):
        normed_g = group_rows(normed, group)
        sum_gate = sum_gate + rounded(jnp.dot(normed_g.T, group_rows(grad_gate_h, group), preferred_element_type=jnp.float32))
        sum_up = sum_up + rounded(jnp.dot(normed_g.T, group_rows(grad_up_h, group), preferred_element_type=jnp.float32))
        sum_down = sum_down + rounded(jnp.dot(group_rows(hidden, group).T, group_rows(cotangent, group), preferred_element_type=jnp.float32))
    return (output, grad_tokens, grad_gain, sum_gate.astype(jnp.bfloat16), sum_up.astype(jnp.bfloat16), sum_down.astype(jnp.bfloat16))
```

```python
import jax
import jax.numpy as jnp
from jax import lax
from jax.sharding import PartitionSpec as P

D = 4096
EPS = 1e-05
FS = 448
CHUNKS = ((0, 448),)


BF = jnp.bfloat16
F32 = jnp.float32


def perm_x(k):
    return [(r, ((r // 2 + k) % 4) * 2 + r % 2) for r in range(8)]


PERM_ZH = [(r, r ^ 1) for r in range(8)]


def perm_zl(k):
    return [(c, ((c // 2 + k) % 4) * 2 + c % 2) for c in range(8)]


PERM_CORE = [(c, c ^ 1) for c in range(8)]


def perm_y(k):
    return [(d, (d + k) % 4) for d in range(4)]


def send_x(v, k):
    return lax.ppermute(v, "row", perm_x(k))


def send_zh(v):
    return lax.ppermute(v, "row", PERM_ZH)


def send_zl(v, k):
    return lax.ppermute(v, "col", perm_zl(k))


def send_core(v):
    return lax.ppermute(v, "col", PERM_CORE)


def send_y(v, k):
    return lax.ppermute(v, "depth", perm_y(k))


def dot(left, right, dims):
    return lax.dot_general(left, right, (dims, ((), ())), preferred_element_type=F32)


def split(value):
    hi = value.astype(BF)
    lo = (value - hi.astype(F32)).astype(BF)
    return hi, lo


def body(tokens, norm_gain, w_gate, w_up, w_down, cotangent):
    x_at = lax.axis_index("row") // 2
    depth_at = lax.axis_index("depth")
    gain = norm_gain[None, :]

    both = jnp.concatenate([tokens, cotangent], axis=1)
    both = jnp.concatenate([both] + [send_y(both, k) for k in (1, -1, 2)], axis=0)
    both = jnp.concatenate([both] + [send_zl(both, k) for k in (1, 2, 3)], axis=0)
    both = jnp.concatenate([both, send_core(both)], axis=0)
    x_all = both[:, :512]
    cot_all = both[:, 512:]
    x_f32 = x_all.astype(F32)
    u_all = (x_f32 * gain).astype(BF)

    chunks = []
    for at, size in CHUNKS:
        start = depth_at * FS + at
        wg = lax.dynamic_slice(w_gate, (0, start), (512, size))
        wu = lax.dynamic_slice(w_up, (0, start), (512, size))
        wd = lax.dynamic_slice(w_down, (start, 0), (size, 512))
        chunks.append((at, size, wg, wu, wd))

    def block(array, k):
        return lax.dynamic_slice(array, (((x_at + k) % 4) * 256, 0), (256, array.shape[1]))

    inv = None
    mixed = jnp.zeros((1024, 512), F32)
    g_all = jnp.zeros((1024, 512), F32)
    grads = []
    for number, (at, size, wg, wu, wd) in enumerate(chunks):
        def partial(k):
            xb = block(x_all, k)
            ub = (xb.astype(F32) * gain).astype(BF)
            parts = [dot(ub, wg, ((1,), (0,))), dot(ub, wu, ((1,), (0,))), dot(block(cot_all, k), wd, ((1,), (1,)))]
            if number == 0:
                xf = xb.astype(F32)
                parts.append(jnp.sum(xf * xf, axis=1, keepdims=True))
            return parts

        def pack(parts):
            out = [p.astype(BF) for p in parts[:3]]
            if number == 0:
                out += list(split(parts[3]))
            return jnp.concatenate(out, axis=1)

        def unpack(message):
            m = message.astype(F32)
            out = [m[:, :size], m[:, size:2 * size], m[:, 2 * size:3 * size]]
            if number == 0:
                out.append(m[:, 3 * size:3 * size + 1] + m[:, 3 * size + 1:3 * size + 2])
            return out

        received = [unpack(send_x(pack(partial(k)), k)) for k in (2, 1, -1)]
        total = partial(0)
        for other in received:
            total = [a + b for a, b in zip(total, other)]
        other = unpack(send_zh(pack(total)))
        total = [a + b for a, b in zip(total, other)]
        if number == 0:
            inv = lax.rsqrt(total[3] / D + EPS)
        gate = total[0] * inv
        up = total[1] * inv
        grad_hidden = total[2]
        sig = jax.nn.sigmoid(gate)
        act = gate * sig
        hidden = (act * up).astype(BF)
        scaled = inv * grad_hidden
        grad_up = (scaled * act).astype(BF)
        grad_gate = (scaled * up * sig * (1.0 + gate * (1.0 - sig))).astype(BF)
        mine = jnp.concatenate([hidden, grad_gate, grad_up], axis=1)
        whole = jnp.zeros((1024, 3 * size), BF)
        for k, piece in [(0, mine)] + [(k, send_x(mine, k)) for k in (2, 1, -1)]:
            whole = lax.dynamic_update_slice(whole, piece, (((x_at - k) % 4) * 256, 0))
        hid = whole[:, :size]
        gg = whole[:, size:2 * size]
        gu = whole[:, 2 * size:]
        mixed = mixed + dot(hid, wd, ((1,), (0,)))
        g_all = g_all + dot(gg, wg, ((1,), (1,))) + dot(gu, wu, ((1,), (1,)))
        d_gu = dot(u_all, whole[:, size:], ((0,), (0,))).astype(BF)
        d_down = dot(hid, cot_all, ((0,), (0,))).astype(BF)
        grads.append((at, size, d_gu, d_down))

    gain_part = jnp.sum(g_all * x_f32, axis=0)[None, :]

    def with_row(rows, vector):
        return jnp.concatenate([rows.astype(BF), jnp.concatenate(split(vector), axis=1)], axis=0)

    def without_row(message):
        m = message.astype(F32)
        return m[:-1], m[-1:, :512] + m[-1:, 512:]

    part = jnp.concatenate([mixed, g_all], axis=1)
    rows, vec = without_row(send_core(with_row(part[512:], gain_part)))
    part = part[:512] + rows
    gain_part = gain_part + vec
    messages = [(k, send_zl(with_row(part[128 * k:128 * (k + 1)], gain_part), -k)) for k in (2, 1, 3)]
    part = part[:128]
    for _, message in messages:
        rows, vec = without_row(message)
        part = part + rows
        gain_part = gain_part + vec
    messages = [send_y(with_row(part[32 * i:32 * (i + 1)], gain_part), k) for i, k in ((1, -1), (2, 1), (3, 2))]
    part = part[:32]
    for message in messages:
        rows, vec = without_row(message)
        part = part + rows
        gain_part = gain_part + vec
    inputs = tokens.astype(F32)
    output = (inputs + part[:, :512]).astype(BF)
    g_own = part[:, 512:]
    stats = jnp.stack([jnp.sum(inputs * inputs, axis=1), jnp.sum(g_own * gain * inputs, axis=1)])
    stats = stats + send_x(stats, 1) + send_x(stats, -1) + send_x(stats, 2)
    stats = stats + send_zh(stats)
    inv_own = lax.rsqrt(stats[0] / D + EPS)[:, None]
    proj = stats[1][:, None]
    grad_tokens = (
        cotangent.astype(F32) + g_own * gain - inputs * (inv_own * inv_own * (proj / D))
    ).astype(BF)
    grad_gain = gain_part[0]

    out_gate = jnp.zeros((512, 4 * FS), BF)
    out_up = jnp.zeros((512, 4 * FS), BF)
    out_down = jnp.zeros((4 * FS, 512), BF)
    for at, size, d_gu, d_down in grads:
        gu_prev, gu_next = send_y(d_gu, 1), send_y(d_gu, -1)
        dn_prev, dn_next = send_y(d_down, 1), send_y(d_down, -1)
        half = size // 2
        gu_far = jnp.concatenate([send_y(gu_prev[:256], 1), send_y(gu_next[256:], -1)], axis=0)
        dn_far = jnp.concatenate([send_y(dn_prev[:half], 1), send_y(dn_next[half:], -1)], axis=0)
        for k, gu, dn in ((0, d_gu, d_down), (-1, gu_prev, dn_prev), (1, gu_next, dn_next), (2, gu_far, dn_far)):
            start = ((depth_at + k) % 4) * FS + at
            out_gate = lax.dynamic_update_slice(out_gate, gu[:, :size], (0, start))
            out_up = lax.dynamic_update_slice(out_up, gu[:, size:], (0, start))
            out_down = lax.dynamic_update_slice(out_down, dn, (start, 0))
    return output, grad_tokens, grad_gain, out_gate, out_up, out_down


def solution(mesh):
    in_specs = (
        P(("col", "depth"), "row"),
        P("row"),
        P("row", "col"),
        P("row", "col"),
        P("col", "row"),
        P(("col", "depth"), "row"),
    )
    out_specs = (
        P(("col", "depth"), "row"),
        P(("col", "depth"), "row"),
        P("row"),
        P("row", "col"),
        P("row", "col"),
        P("col", "row"),
    )
    return jax.shard_map(body, mesh=mesh, in_specs=in_specs, out_specs=out_specs, check_vma=False)
```

```python
import jax
import jax.numpy as jnp
from jax import lax
from jax.experimental import pallas as pl
from jax.experimental.pallas import tpu as pltpu
from jax.sharding import PartitionSpec as P


D = 4096
EPS = 1e-05
FS = 448
CHUNKS = ((0, 224), (224, 224))


BF = jnp.bfloat16
F32 = jnp.float32


def perm_x(k):
    return [(r, ((r // 2 + k) % 4) * 2 + r % 2) for r in range(8)]


PERM_ZH = [(r, r ^ 1) for r in range(8)]


def perm_zl(k):
    return [(c, ((c // 2 + k) % 4) * 2 + c % 2) for c in range(8)]


PERM_CORE = [(c, c ^ 1) for c in range(8)]


def perm_y(k):
    return [(d, (d + k) % 4) for d in range(4)]


def send(v, axis, perm):
    return lax.ppermute(v, axis, perm)


def send_x(v, k):
    return send(v, "row", perm_x(k))


def send_zh(v):
    return send(v, "row", PERM_ZH)


def send_zl(v, k):
    return send(v, "col", perm_zl(k))


def send_core(v):
    return send(v, "col", PERM_CORE)


def send_y(v, k):
    return send(v, "depth", perm_y(k))


def nt(left, right):
    return lax.dot_general(left, right, (((1,), (1,)), ((), ())), preferred_element_type=F32)


def nn(left, right):
    return lax.dot_general(left, right, (((1,), (0,)), ((), ())), preferred_element_type=F32)


def tn(left, right):
    return lax.dot_general(left, right, (((0,), (0,)), ((), ())), preferred_element_type=F32)


VM = pl.BlockSpec(memory_space=pltpu.VMEM)
SM = pl.BlockSpec(memory_space=pltpu.SMEM)


def sds(shape, dtype):
    return jax.ShapeDtypeStruct(shape, dtype)


ANY = pl.BlockSpec(memory_space=pl.ANY)


def call(kernel, outs, scalars, *args, scratch=(), raw=0, hbm_in=(), hbm_out=(), limit=12):
    outs = [o if i in hbm_out else pltpu.VMEM(o.shape, o.dtype) for i, o in enumerate(outs)]
    run = pl.pallas_call(
        kernel,
        out_shape=outs,
        in_specs=[SM] * len(scalars) + [ANY] * raw + [VM] * (len(args) - raw),
        out_specs=[VM] * len(outs),
        scratch_shapes=list(scratch),
        compiler_params=pltpu.CompilerParams(vmem_limit_bytes=limit << 20),
    )
    placed = [
        a if i < raw or i in hbm_in else pltpu.with_memory_space_constraint(a, pltpu.VMEM)
        for i, a in enumerate(args)
    ]
    return run(*scalars, *placed)


def split(value):
    hi = value.astype(BF)
    return hi, (value - hi.astype(F32)).astype(BF)


def add_stat(message, size):
    return message[3 * size:3 * size + 8, :].astype(F32) + message[3 * size + 8:, :].astype(F32)


def pack_call(tokens, cotangent):
    def kernel(tok_ref, cot_ref, out_ref):
        out_ref[:, :512] = tok_ref[...]
        out_ref[:, 512:] = cot_ref[...]

    return call(kernel, [sds((32, 1024), BF)], (), tokens, cotangent, hbm_in=(0, 1))[0]


def prepare_call(depth_at, w_gate, w_up, w_down):
    def kernel(at_ref, gate_ref, up_ref, down_ref, *refs):
        outs, (cut_ref, turned_ref, sems) = refs[:-3], refs[-3:]
        at = at_ref[0]
        start = pl.multiple_of(((7 * at) // 2) * 128, 128)
        skip = pl.multiple_of((at % 2) * 64, 64)
        copies = [
            pltpu.make_async_copy(ref.at[:, pl.ds(start, 512)], cut_ref.at[i], sems.at[i])
            for i, ref in enumerate((gate_ref, up_ref))
        ]
        for i, (where, size) in enumerate(CHUNKS):
            rows = pl.ds(pl.multiple_of(at * FS + where, 16), size)
            copies.append(pltpu.make_async_copy(down_ref.at[rows, :], outs[2 * i + 1], sems.at[2 + i]))
        for copy in copies:
            copy.start()
        for which in (0, 1):
            copies[which].wait()
            turned_ref[which] = cut_ref[which].T
            for i, (where, size) in enumerate(CHUNKS):
                outs[2 * i][which * size:(which + 1) * size, :] = turned_ref[which, pl.ds(skip + where, size), :]
        for copy in copies[2:]:
            copy.wait()

    outs = []
    for _, size in CHUNKS:
        outs += [sds((2 * size, 512), BF), sds((size, 512), BF)]
    scratch = [pltpu.VMEM((2, 512, 512), BF), pltpu.VMEM((2, 512, 512), BF), pltpu.SemaphoreType.DMA((4,))]
    return call(kernel, outs, (depth_at,), w_gate, w_up, w_down, scratch=scratch, raw=3)


def block_rows(at_ref, k):
    return pl.ds(pl.multiple_of(((at_ref[0] + k + 4) % 4) * 256, 256), 256)


def block_part(rows, both_ref, gain_ref, wgu_ref, wd_ref, first):
    x = both_ref[rows, :512].astype(F32)
    parts = [nt(wgu_ref[...], (x * gain_ref[...]).astype(BF)), nt(wd_ref[...], both_ref[rows, 512:])]
    if first:
        hi, lo = split(x * x)
        ones = jnp.ones((8, 512), BF)
        parts.append(nt(ones, hi) + nt(ones, lo))
    return parts


def write_parts(ref, parts, size):
    ref[:2 * size, :] = parts[0].astype(BF)
    ref[2 * size:3 * size, :] = parts[1].astype(BF)
    if len(parts) > 2:
        hi, lo = split(parts[2])
        ref[3 * size:, :] = jnp.concatenate([hi, lo], axis=0)


def read_parts(ref, size, first):
    parts = [ref[:2 * size, :].astype(F32), ref[2 * size:3 * size, :].astype(F32)]
    if first:
        parts.append(add_stat(ref, size))
    return parts


def message_shape(size, first):
    return sds((3 * size + (16 if first else 0), 256), BF)


def partial_call(x_at, ks, both, gain, wgu, wd, size, first):
    def kernel(at_ref, both_ref, gain_ref, wgu_ref, wd_ref, *outs):
        for k, out_ref in zip(ks, outs):
            write_parts(out_ref, block_part(block_rows(at_ref, k), both_ref, gain_ref, wgu_ref, wd_ref, first), size)

    return call(kernel, [message_shape(size, first)] * len(ks), (x_at,), both, gain, wgu, wd, hbm_in=(1,))


def sum_call(x_at, both, gain, wgu, wd, received, size, first):
    def kernel(at_ref, both_ref, gain_ref, wgu_ref, wd_ref, a_ref, b_ref, c_ref, total_ref, out_ref):
        total = block_part(block_rows(at_ref, 0), both_ref, gain_ref, wgu_ref, wd_ref, first)
        for ref in (a_ref, b_ref, c_ref):
            total = [a + b for a, b in zip(total, read_parts(ref, size, first))]
        total_ref[:2 * size, :] = total[0]
        total_ref[2 * size:3 * size, :] = total[1]
        if first:
            total_ref[3 * size:, :] = total[2]
        write_parts(out_ref, total, size)

    outs = [sds((3 * size + (8 if first else 0), 256), F32), message_shape(size, first)]
    return call(kernel, outs, (x_at,), both, gain, wgu, wd, *received, hbm_in=(1,))


def middle_call(total, other, inv, size):
    first = inv is None

    def kernel(total_ref, other_ref, *refs):
        if first:
            out_ref, inv_ref = refs
            stat = total_ref[3 * size:, :] + add_stat(other_ref, size)
            inv_ref[...] = lax.rsqrt(stat / D + EPS)
        else:
            inv_ref, out_ref = refs
        scale = inv_ref[0:1, :]
        gate = (total_ref[:size, :] + other_ref[:size, :].astype(F32)) * scale
        up = (total_ref[size:2 * size, :] + other_ref[size:2 * size, :].astype(F32)) * scale
        grad = (total_ref[2 * size:3 * size, :] + other_ref[2 * size:3 * size, :].astype(F32)) * scale
        sig = jax.nn.sigmoid(gate)
        act = gate * sig
        out_ref[:size, :] = (act * up).astype(BF)
        out_ref[size:2 * size, :] = (grad * up * sig * (1.0 + gate * (1.0 - sig))).astype(BF)
        out_ref[2 * size:, :] = (grad * act).astype(BF)

    out = sds((3 * size, 256), BF)
    if first:
        return call(kernel, [out, sds((8, 256), F32)], (), total, other)
    return call(kernel, [out], (), total, other, inv)[0], inv


def weight_grad_call(x_at, pieces, both, gain, size):
    def kernel(at_ref, a_ref, b_ref, c_ref, d_ref, both_ref, gain_ref, out_ref):
        down = jnp.zeros((size, 512), F32)
        gate_up = jnp.zeros((2 * size, 512), F32)
        for k, ref in zip((0, 2, 1, -1), (a_ref, b_ref, c_ref, d_ref)):
            rows = block_rows(at_ref, -k)
            u = (both_ref[rows, :512].astype(F32) * gain_ref[...]).astype(BF)
            down = down + nn(ref[:size, :], both_ref[rows, 512:])
            gate_up = gate_up + nn(ref[size:, :], u)
        out_ref[:size, :] = down.astype(BF)
        out_ref[size:, :] = gate_up.astype(BF)

    return call(kernel, [sds((3 * size, 512), BF)], (x_at,), *pieces, both, gain, hbm_in=(5,))[0]


def write_gain(ref, rows, vector):
    hi, lo = split(vector)
    ref[rows:, :512] = jnp.concatenate([hi, hi], axis=0)
    ref[rows:, 512:] = jnp.concatenate([lo, lo], axis=0)


def read_gain(ref, rows):
    return ref[rows:rows + 8, :512].astype(F32) + ref[rows:rows + 8, 512:].astype(F32)


def back_call(x_at, pieces, wgu, wd, before, both, size, last):
    def kernel(at_ref, a_ref, b_ref, c_ref, d_ref, wgu_ref, wd_ref, both_ref, *refs):
        refs = list(refs)
        before_ref = refs.pop(0) if before is not None else None
        if last:
            own_ref, gain_ref, out_ref, acc_ref = refs
        else:
            acc_ref, = refs
        vector = jnp.zeros((1, 512), F32)
        for k, ref in zip((0, 2, 1, -1), (a_ref, b_ref, c_ref, d_ref)):
            rows = block_rows(at_ref, -k)
            mixed = tn(ref[:size, :], wd_ref[...])
            grad = tn(ref[size:, :], wgu_ref[...])
            if before is not None:
                mixed = mixed + before_ref[rows, :512]
                grad = grad + before_ref[rows, 512:]
            acc_ref[rows, :512] = mixed
            acc_ref[rows, 512:] = grad
            if last:
                vector = vector + jnp.sum(grad * both_ref[rows, :512].astype(F32), axis=0, keepdims=True)
        if last:
            own_ref[...] = acc_ref[:512, :]
            out_ref[:512, :] = acc_ref[512:, :].astype(BF)
            vector = jnp.broadcast_to(vector, (8, 512))
            gain_ref[...] = vector
            write_gain(out_ref, 512, vector)

    args = list(pieces) + [wgu, wd, both] + ([before] if before is not None else [])
    if last:
        outs = [sds((512, 1024), F32), sds((8, 512), F32), sds((528, 1024), BF)]
        return call(kernel, outs, (x_at,), *args, scratch=[pltpu.VMEM((1024, 1024), F32)])
    return call(kernel, [sds((1024, 1024), F32)], (x_at,), *args)[0]


def fold_call(own, vector, messages, strips):
    rows = own.shape[0]
    count = len(messages)
    keep = sum(size for _, size in strips[0])

    def kernel(own_ref, vector_ref, *refs):
        received = refs[:count]
        keep_ref, gain_ref = refs[count:count + 2]
        outs = refs[count + 2:]
        vec = vector_ref[...]
        for ref in received:
            vec = vec + read_gain(ref, rows)
        gain_ref[...] = vec
        for strip, out in zip(strips, (keep_ref,) + tuple(outs)):
            to = 0
            for at, size in strip:
                total = own_ref[at:at + size, :]
                for ref in received:
                    total = total + ref[at:at + size, :].astype(F32)
                out[to:to + size, :] = total.astype(out.dtype)
                to += size
        for ref in outs:
            write_gain(ref, keep, vec)

    outs = [sds((keep, 1024), F32), sds((8, 512), F32)] + [sds((keep + 16, 1024), BF)] * (len(strips) - 1)
    return call(kernel, outs, (), own, vector, *messages)


def final_call(own, vector, messages, tokens, gain):
    def kernel(own_ref, vector_ref, a_ref, b_ref, c_ref, tok_ref, gain_ref, out_ref, g_ref, vec_ref, stat_ref):
        total = own_ref[...]
        vec = vector_ref[...]
        for ref in (a_ref, b_ref, c_ref):
            total = total + ref[:32, :].astype(F32)
            vec = vec + read_gain(ref, 32)
        vec_ref[...] = vec[:1, :]
        x = tok_ref[...].astype(F32)
        out_ref[...] = (x + total[:, :512]).astype(BF)
        g = total[:, 512:] * gain_ref[...]
        g_ref[...] = g
        stat_ref[:, :128] = jnp.broadcast_to(jnp.sum(x * x, axis=1, keepdims=True), (32, 128))
        stat_ref[:, 128:] = jnp.broadcast_to(jnp.sum(g * x, axis=1, keepdims=True), (32, 128))

    outs = [sds((32, 512), BF), sds((32, 512), F32), sds((1, 512), F32), sds((32, 256), F32)]
    return call(kernel, outs, (), own, vector, *messages, tokens, gain, hbm_in=(5, 6), hbm_out=(0, 2))


def tail_call(stats, other, cotangent, tokens, g_own):
    def kernel(a_ref, b_ref, cot_ref, tok_ref, g_ref, out_ref):
        stat = a_ref[...] + b_ref[...]
        inv = lax.rsqrt(stat[:, :1] / D + EPS)
        proj = stat[:, 128:129]
        x = tok_ref[...].astype(F32)
        out_ref[...] = (cot_ref[...].astype(F32) + g_ref[...] - x * (inv * inv * (proj / D))).astype(BF)

    return call(kernel, [sds((32, 512), BF)], (), stats, other, cotangent, tokens, g_own, hbm_in=(2, 3), hbm_out=(0,))[0]


def add_call(parts):
    def kernel(a_ref, b_ref, c_ref, d_ref, out_ref):
        out_ref[...] = a_ref[...] + b_ref[...] + c_ref[...] + d_ref[...]

    return call(kernel, [sds(parts[0].shape, F32)], (), *parts)[0]


def assemble_call(depth_at, groups):
    count = len(groups)

    def kernel(at_ref, *refs):
        gate_ref, up_ref, down_ref, tgate_ref, tup_ref = refs[5 * count:]
        for i, (at, size, _) in enumerate(groups):
            own, prev, after, far_a, far_b = refs[5 * i:5 * i + 5]
            half = 3 * size // 2
            for k, ref in ((0, own), (3, prev), (1, after)):
                start = ((at_ref[0] + k) % 4) * FS + at
                rows = pl.ds(pl.multiple_of(start, 16), size)
                down_ref[rows, :] = ref[:size, :]
                tgate_ref[rows, :] = ref[size:2 * size, :]
                tup_ref[rows, :] = ref[2 * size:, :]
            start = ((at_ref[0] + 2) % 4) * FS + at
            rows = pl.ds(pl.multiple_of(start, 16), size)
            down_ref[rows, :] = far_a[:size, :]
            tgate_ref[pl.ds(pl.multiple_of(start, 16), half - size), :] = far_a[size:, :]
            tgate_ref[pl.ds(pl.multiple_of(start + half - size, 16), 2 * size - half), :] = far_b[:2 * size - half, :]
            tup_ref[rows, :] = far_b[2 * size - half:, :]

        def turn(i, carry):
            cut = pl.ds(pl.multiple_of(i * 128, 128), 128)
            gate_ref[:, cut] = tgate_ref[cut, :].T
            up_ref[:, cut] = tup_ref[cut, :].T
            return carry

        lax.fori_loop(0, 14, turn, 0)

    args = [a for g in groups for a in g[2]]
    outs = [sds((512, 4 * FS), BF), sds((512, 4 * FS), BF), sds((4 * FS, 512), BF)]
    scratch = [pltpu.VMEM((4 * FS, 512), BF), pltpu.VMEM((4 * FS, 512), BF)]
    return call(kernel, outs, (depth_at,), *args, scratch=scratch, hbm_out=(0, 1, 2), limit=24)


def step(tokens, norm_gain, w_gate, w_up, w_down, cotangent):
    x_at = jnp.reshape(lax.axis_index("row") // 2, (1,)).astype(jnp.int32)
    depth_at = jnp.reshape(lax.axis_index("depth"), (1,)).astype(jnp.int32)
    gain = norm_gain[None, :]
    count = len(CHUNKS)

    both = pack_call(tokens, cotangent)
    near = [send_zl(both, k) for k in (1, 2, 3)]
    weights = prepare_call(depth_at, w_gate, w_up, w_down)
    both = jnp.concatenate([both] + near, axis=0)
    both = jnp.concatenate([both] + [send_y(both, k) for k in (1, -1, 2)], axis=0)
    both = jnp.concatenate([both, send_core(both)], axis=0)
    chunks = [(at, size, weights[2 * i], weights[2 * i + 1]) for i, (at, size) in enumerate(CHUNKS)]

    received = []
    for n, (at, size, wgu, wd) in enumerate(chunks):
        groups = [(2,), (1,), (-1,)] if n == 0 else [(2, 1, -1)]
        arrived = []
        for ks in groups:
            parts = partial_call(x_at, ks, both, gain, wgu, wd, size, n == 0)
            arrived += [send_x(part, k) for k, part in zip(ks, parts)]
        received.append(arrived)
    halves = []
    for n, (at, size, wgu, wd) in enumerate(chunks):
        total, message = sum_call(x_at, both, gain, wgu, wd, received[n], size, n == 0)
        halves.append((total, send_zh(message)))
    inv = None
    pieces = []
    for n, (at, size, wgu, wd) in enumerate(chunks):
        mine, inv = middle_call(*halves[n], inv, size)
        pieces.append([mine] + [send_x(mine, k) for k in (2, 1, -1)])

    def weight_grad(n):
        at, size, _, _ = chunks[n]
        grad = weight_grad_call(x_at, pieces[n], both, gain, size)
        return at, size, grad, send_y(grad, 1), send_y(grad, -1)

    def relay(at, size, grad, prev, after):
        half = 3 * size // 2
        return at, size, [grad, prev, after, send_y(prev[:half], 1), send_y(after[half:], -1)]

    def back(n, before):
        _, size, wgu, wd = chunks[n]
        return back_call(x_at, pieces[n], wgu, wd, before, both, size, n == count - 1)

    grads = []
    before = None
    for n in range(count - 1):
        grads.append(weight_grad(n))
        before = back(n, before)
    own, vector, message = back(count - 1, before)
    message = send_core(message)
    groups = [relay(*g) for g in grads]
    last = weight_grad(count - 1)
    strips = [[(128 * a + 32 * j, 32) for a in range(4)] for j in range(4)]
    own, vector, *messages = fold_call(own, vector, [message], strips)
    messages = [send_zl(m, -k) for k, m in zip((1, 2, 3), messages)]
    own, vector, *messages = fold_call(own, vector, messages, [[(32 * j, 32)] for j in range(4)])
    messages = [send_y(m, k) for k, m in zip((-1, 1, 2), messages)]
    groups.append(relay(*last))
    output, g_own, vector, stats = final_call(own, vector, messages, tokens, gain)
    stats = add_call([stats] + [send_x(stats, k) for k in (1, -1, 2)])
    grad_tokens = tail_call(stats, send_zh(stats), cotangent, tokens, g_own)
    out_gate, out_up, out_down = assemble_call(depth_at, groups)
    return output, grad_tokens, vector[0], out_gate, out_up, out_down


def solution(mesh):
    in_specs = (
        P(("col", "depth"), "row"),
        P("row"),
        P("row", "col"),
        P("row", "col"),
        P("col", "row"),
        P(("col", "depth"), "row"),
    )
    out_specs = (
        P(("col", "depth"), "row"),
        P(("col", "depth"), "row"),
        P("row"),
        P("row", "col"),
        P("row", "col"),
        P("col", "row"),
    )
    function = jax.shard_map(step, mesh=mesh, in_specs=in_specs, out_specs=out_specs, check_vma=False)
    shapes = [((1024, D), BF), ((D,), F32), ((D, 32 * FS), BF), ((D, 32 * FS), BF), ((32 * FS, D), BF), ((1024, D), BF)]
    jax.eval_shape(function, *[sds(*shape) for shape in shapes])
    return function
```

```python
import jax
import jax.numpy as jnp
from jax import lax
from jax.experimental import pallas as pl
from jax.experimental.pallas import tpu as pltpu
from jax.sharding import PartitionSpec as P


D = 4096
EPS = 1e-05
FS = 448
CHUNKS = ((0, 224), (224, 224))


BF = jnp.bfloat16
F32 = jnp.float32


def perm_x(k):
    return [(r, ((r // 2 + k) % 4) * 2 + r % 2) for r in range(8)]


PERM_ZH = [(r, r ^ 1) for r in range(8)]


def perm_zl(k):
    return [(c, ((c // 2 + k) % 4) * 2 + c % 2) for c in range(8)]


PERM_CORE = [(c, c ^ 1) for c in range(8)]


def perm_y(k):
    return [(d, (d + k) % 4) for d in range(4)]


def send(v, axis, perm):
    return lax.ppermute(v, axis, perm)


def send_x(v, k):
    return send(v, "row", perm_x(k))


def send_zh(v):
    return send(v, "row", PERM_ZH)


def send_zl(v, k):
    return send(v, "col", perm_zl(k))


def send_core(v):
    return send(v, "col", PERM_CORE)


def send_y(v, k):
    return send(v, "depth", perm_y(k))


def nt(left, right):
    return lax.dot_general(left, right, (((1,), (1,)), ((), ())), preferred_element_type=F32)


def nn(left, right):
    return lax.dot_general(left, right, (((1,), (0,)), ((), ())), preferred_element_type=F32)


def tn(left, right):
    return lax.dot_general(left, right, (((0,), (0,)), ((), ())), preferred_element_type=F32)


VM = pl.BlockSpec(memory_space=pltpu.VMEM)
SM = pl.BlockSpec(memory_space=pltpu.SMEM)


def sds(shape, dtype):
    return jax.ShapeDtypeStruct(shape, dtype)


ANY = pl.BlockSpec(memory_space=pl.ANY)


def call(kernel, outs, scalars, *args, scratch=(), raw=0, hbm_in=(), hbm_out=(), limit=12):
    outs = [o if i in hbm_out else pltpu.VMEM(o.shape, o.dtype) for i, o in enumerate(outs)]
    run = pl.pallas_call(
        kernel,
        out_shape=outs,
        in_specs=[SM] * len(scalars) + [ANY] * raw + [VM] * (len(args) - raw),
        out_specs=[VM] * len(outs),
        scratch_shapes=list(scratch),
        compiler_params=pltpu.CompilerParams(vmem_limit_bytes=limit << 20),
    )
    placed = [
        pltpu.with_memory_space_constraint(a, pltpu.HBM if i < raw or i in hbm_in else pltpu.VMEM)
        for i, a in enumerate(args)
    ]
    return run(*scalars, *placed)


def split(value):
    hi = value.astype(BF)
    return hi, (value - hi.astype(F32)).astype(BF)


def add_stat(message, size):
    return message[3 * size:3 * size + 8, :].astype(F32) + message[3 * size + 8:, :].astype(F32)


def pack_call(tokens, cotangent):
    def kernel(tok_ref, cot_ref, out_ref):
        out_ref[:, :512] = tok_ref[...]
        out_ref[:, 512:] = cot_ref[...]

    return call(kernel, [sds((32, 1024), BF)], (), tokens, cotangent, hbm_in=(0, 1))[0]


def join_call(parts):
    rows = parts[0].shape[0]

    def kernel(*refs):
        for i, ref in enumerate(refs[:-1]):
            refs[-1][rows * i:rows * (i + 1), :] = ref[...]

    return call(kernel, [sds((rows * len(parts), 1024), BF)], (), *parts)[0]


def prepare_call(depth_at, w_gate, w_up, w_down):
    def kernel(at_ref, gate_ref, up_ref, down_ref, *refs):
        outs, (cut_ref, turned_ref, sems) = refs[:-3], refs[-3:]
        at = at_ref[0]
        start = pl.multiple_of(((7 * at) // 2) * 128, 128)
        skip = pl.multiple_of((at % 2) * 64, 64)
        copies = [
            pltpu.make_async_copy(ref.at[:, pl.ds(start, 512)], cut_ref.at[i], sems.at[i])
            for i, ref in enumerate((gate_ref, up_ref))
        ]
        for i, (where, size) in enumerate(CHUNKS):
            rows = pl.ds(pl.multiple_of(at * FS + where, 16), size)
            copies.append(pltpu.make_async_copy(down_ref.at[rows, :], outs[2 * i + 1], sems.at[2 + i]))
        for copy in copies:
            copy.start()
        for which in (0, 1):
            copies[which].wait()
            turned_ref[which] = cut_ref[which].T
            for i, (where, size) in enumerate(CHUNKS):
                outs[2 * i][which * size:(which + 1) * size, :] = turned_ref[which, pl.ds(skip + where, size), :]
        for copy in copies[2:]:
            copy.wait()

    outs = []
    for _, size in CHUNKS:
        outs += [sds((2 * size, 512), BF), sds((size, 512), BF)]
    scratch = [pltpu.VMEM((2, 512, 512), BF), pltpu.VMEM((2, 512, 512), BF), pltpu.SemaphoreType.DMA((4,))]
    return call(kernel, outs, (depth_at,), w_gate, w_up, w_down, scratch=scratch, raw=3)


def block_rows(at_ref, k):
    return pl.ds(pl.multiple_of(((at_ref[0] + k + 4) % 4) * 256, 256), 256)


def block_part(rows, both_ref, gain_ref, wgu_ref, wd_ref, first):
    x = both_ref[rows, :512].astype(F32)
    parts = [nt(wgu_ref[...], (x * gain_ref[...]).astype(BF)), nt(wd_ref[...], both_ref[rows, 512:])]
    if first:
        hi, lo = split(x * x)
        ones = jnp.ones((8, 512), BF)
        parts.append(nt(ones, hi) + nt(ones, lo))
    return parts


def write_parts(ref, parts, size):
    ref[:2 * size, :] = parts[0].astype(BF)
    ref[2 * size:3 * size, :] = parts[1].astype(BF)
    if len(parts) > 2:
        hi, lo = split(parts[2])
        ref[3 * size:, :] = jnp.concatenate([hi, lo], axis=0)


def read_parts(ref, size, first):
    parts = [ref[:2 * size, :].astype(F32), ref[2 * size:3 * size, :].astype(F32)]
    if first:
        parts.append(add_stat(ref, size))
    return parts


def message_shape(size, first):
    return sds((3 * size + (16 if first else 0), 256), BF)


def partial_call(x_at, ks, both, gain, wgu, wd, size, first):
    def kernel(at_ref, both_ref, gain_ref, wgu_ref, wd_ref, *outs):
        for k, out_ref in zip(ks, outs):
            write_parts(out_ref, block_part(block_rows(at_ref, k), both_ref, gain_ref, wgu_ref, wd_ref, first), size)

    return call(kernel, [message_shape(size, first)] * len(ks), (x_at,), both, gain, wgu, wd)


def sum_call(x_at, both, gain, wgu, wd, received, size, first):
    def kernel(at_ref, both_ref, gain_ref, wgu_ref, wd_ref, a_ref, b_ref, c_ref, total_ref, out_ref):
        total = block_part(block_rows(at_ref, 0), both_ref, gain_ref, wgu_ref, wd_ref, first)
        for ref in (a_ref, b_ref, c_ref):
            total = [a + b for a, b in zip(total, read_parts(ref, size, first))]
        total_ref[:2 * size, :] = total[0]
        total_ref[2 * size:3 * size, :] = total[1]
        if first:
            total_ref[3 * size:, :] = total[2]
        write_parts(out_ref, total, size)

    outs = [sds((3 * size + (8 if first else 0), 256), F32), message_shape(size, first)]
    return call(kernel, outs, (x_at,), both, gain, wgu, wd, *received)


def middle_call(total, other, inv, size):
    first = inv is None

    def kernel(total_ref, other_ref, *refs):
        if first:
            out_ref, inv_ref = refs
            stat = total_ref[3 * size:, :] + add_stat(other_ref, size)
            inv_ref[...] = lax.rsqrt(stat / D + EPS)
        else:
            inv_ref, out_ref = refs
        scale = inv_ref[0:1, :]
        gate = (total_ref[:size, :] + other_ref[:size, :].astype(F32)) * scale
        up = (total_ref[size:2 * size, :] + other_ref[size:2 * size, :].astype(F32)) * scale
        grad = (total_ref[2 * size:3 * size, :] + other_ref[2 * size:3 * size, :].astype(F32)) * scale
        sig = jax.nn.sigmoid(gate)
        act = gate * sig
        out_ref[:size, :] = (act * up).astype(BF)
        grad_gate = grad * up * sig * (1.0 + gate * (1.0 - sig))
        grad_up = grad * act
        out_ref[size:2 * size, :] = grad_gate.astype(BF)
        out_ref[2 * size:3 * size, :] = grad_up.astype(BF)
        inner = jnp.sum(grad_gate * gate + grad_up * up, axis=0, keepdims=True)
        hi, lo = split(jnp.broadcast_to(inner, (8, 256)))
        out_ref[3 * size:3 * size + 16, :] = jnp.concatenate([hi, lo], axis=0)
        if first:
            hi, lo = split(inv_ref[...])
            out_ref[3 * size + 16:, :] = jnp.concatenate([hi, lo], axis=0)

    out = sds((3 * size + (32 if first else 16), 256), BF)
    if first:
        return call(kernel, [out, sds((8, 256), F32)], (), total, other)
    return call(kernel, [out], (), total, other, inv)[0], inv


def weight_grad_call(x_at, pieces, both, gain, size):
    def kernel(at_ref, a_ref, b_ref, c_ref, d_ref, both_ref, gain_ref, out_ref):
        down = jnp.zeros((size, 512), F32)
        gate_up = jnp.zeros((2 * size, 512), F32)
        for k, ref in zip((0, 2, 1, -1), (a_ref, b_ref, c_ref, d_ref)):
            rows = block_rows(at_ref, -k)
            u = (both_ref[rows, :512].astype(F32) * gain_ref[...]).astype(BF)
            down = down + nn(ref[:size, :], both_ref[rows, 512:])
            gate_up = gate_up + nn(ref[size:3 * size, :], u)
        out_ref[:size, :] = down.astype(BF)
        out_ref[size:, :] = gate_up.astype(BF)

    return call(kernel, [sds((3 * size, 512), BF)], (x_at,), *pieces, both, gain)[0]


def write_extra(ref, rows, gain_part, inner):
    gain_hi, gain_lo = split(gain_part)
    inner_hi, inner_lo = split(inner)
    ref[rows:, :512] = jnp.concatenate([gain_hi, inner_hi], axis=0)
    ref[rows:, 512:] = jnp.concatenate([gain_lo, inner_lo], axis=0)


def read_extra(ref, rows):
    extra = ref[rows:, :].astype(F32)
    extra = extra[:, :512] + extra[:, 512:]
    return extra[:8, :], extra[8:, :]


def read_pair(ref, at):
    return ref[at:at + 8, :].astype(F32) + ref[at + 8:at + 16, :].astype(F32)


def back_call(x_at, pieces, wgu, wd, before, both, size, last):
    first = before is None

    def kernel(at_ref, a_ref, b_ref, c_ref, d_ref, wgu_ref, wd_ref, both_ref, *refs):
        refs = list(refs)
        if not first:
            before_ref, before_inner_ref = refs.pop(0), refs.pop(0)
        if last:
            own_ref, gain_ref, own_inner_ref, out_ref, acc_ref, inner_ref = refs
        else:
            acc_ref, inner_ref, inv_ref, all_inv_ref = refs
        gain_part = jnp.zeros((1, 512), F32)
        for k, ref in zip((0, 2, 1, -1), (a_ref, b_ref, c_ref, d_ref)):
            rows = block_rows(at_ref, -k)
            mixed = tn(ref[:size, :], wd_ref[...])
            grad = tn(ref[size:3 * size, :], wgu_ref[...])
            inner = read_pair(ref, 3 * size)
            if not first:
                mixed = mixed + before_ref[rows, :512]
                grad = grad + before_ref[rows, 512:]
                inner = inner + before_inner_ref[:, rows]
            acc_ref[rows, :512] = mixed
            acc_ref[rows, 512:] = grad
            inner_ref[:, rows] = inner
            if first:
                all_inv_ref[:, rows] = read_pair(ref, 3 * size + 16)
            if last:
                gain_part = gain_part + jnp.sum(grad * both_ref[rows, :512].astype(F32), axis=0, keepdims=True)
        if first:
            inv_ref[...] = all_inv_ref[:, :128]
        if last:
            own_ref[...] = acc_ref[:512, :]
            own_inner_ref[...] = inner_ref[:, :512]
            out_ref[:512, :] = acc_ref[512:, :].astype(BF)
            gain_part = jnp.broadcast_to(gain_part, (8, 512))
            gain_ref[...] = gain_part
            write_extra(out_ref, 512, gain_part, inner_ref[:, 512:])

    args = list(pieces) + [wgu, wd, both] + ([] if first else list(before))
    acc, inner = sds((1024, 1024), F32), sds((8, 1024), F32)
    if last:
        outs = [sds((512, 1024), F32), sds((8, 512), F32), sds((8, 512), F32), sds((528, 1024), BF)]
        scratch = [pltpu.VMEM(acc.shape, F32), pltpu.VMEM(inner.shape, F32)]
        return call(kernel, outs, (x_at,), *args, scratch=scratch)
    return call(kernel, [acc, inner, sds((8, 128), F32)], (x_at,), *args, scratch=[pltpu.VMEM((8, 1024), F32)])


def turn_left(inner, lanes):
    if not lanes:
        return inner
    return jnp.concatenate(
        [pltpu.roll(inner[:, 128 * i:128 * (i + 1)], 128 - lanes, 1) for i in range(4)], axis=1)


def fold_call(own, gain_part, inner, messages, turns, strips):
    rows = own.shape[0]
    count = len(messages)
    keep = sum(size for _, size in strips[0])

    def kernel(own_ref, gain_ref, inner_ref, *refs):
        received = refs[:count]
        keep_ref, gain_out_ref, inner_out_ref = refs[count:count + 3]
        outs = refs[count + 3:]
        gain_sum, inner_sum = gain_ref[...], inner_ref[...]
        for ref, lanes in zip(received, turns):
            gain_more, inner_more = read_extra(ref, rows)
            gain_sum = gain_sum + gain_more
            inner_sum = inner_sum + turn_left(inner_more, lanes)
        gain_out_ref[...] = gain_sum
        inner_out_ref[...] = inner_sum
        for strip, out in zip(strips, (keep_ref,) + tuple(outs)):
            to = 0
            for at, size in strip:
                total = own_ref[at:at + size, :]
                for ref in received:
                    total = total + ref[at:at + size, :].astype(F32)
                out[to:to + size, :] = total.astype(out.dtype)
                to += size
        for ref in outs:
            write_extra(ref, keep, gain_sum, inner_sum)

    outs = [sds((keep, 1024), F32), sds((8, 512), F32), sds((8, 512), F32)]
    outs += [sds((keep + 16, 1024), BF)] * (len(strips) - 1)
    return call(kernel, outs, (), own, gain_part, inner, *messages)


def as_column(rows):
    hi, lo = split(rows)
    eighth = jnp.full((16, 128), 0.125, BF)
    return tn(jnp.concatenate([hi, lo], axis=0), eighth)[:32, :1]


def final_call(own, gain_part, inner, inv, messages, tokens, cotangent, gain):
    def kernel(own_ref, part_ref, inner_ref, inv_ref, a_ref, b_ref, c_ref, tok_ref, cot_ref, gain_ref, out_ref, grad_ref, vec_ref):
        total = own_ref[...]
        gain_sum, inner_sum = part_ref[...], inner_ref[:, :128]
        for i, ref in enumerate((a_ref, b_ref, c_ref)):
            total = total + ref[:32, :].astype(F32)
            gain_more, inner_more = read_extra(ref, 32)
            gain_sum = gain_sum + gain_more
            inner_sum = inner_sum + inner_more[:, 128 * (i + 1):128 * (i + 2)]
        vec_ref[...] = gain_sum[:1, :]
        x = tok_ref[...].astype(F32)
        out_ref[...] = (x + total[:, :512]).astype(BF)
        scale = as_column(inv_ref[...]) * (as_column(inner_sum) / D)
        grad_ref[...] = (cot_ref[...].astype(F32) + total[:, 512:] * gain_ref[...] - x * scale).astype(BF)

    outs = [sds((32, 512), BF), sds((32, 512), BF), sds((1, 512), F32)]
    return call(kernel, outs, (), own, gain_part, inner, inv, *messages, tokens, cotangent, gain, hbm_out=(0, 1, 2))


def assemble_call(depth_at, groups):
    count = len(groups)

    def kernel(at_ref, *refs):
        gate_ref, up_ref, down_ref, tgate_ref, tup_ref = refs[5 * count:]
        for i, (at, size, _) in enumerate(groups):
            own, prev, after, far_a, far_b = refs[5 * i:5 * i + 5]
            half = 3 * size // 2
            for k, ref in ((0, own), (3, prev), (1, after)):
                start = ((at_ref[0] + k) % 4) * FS + at
                rows = pl.ds(pl.multiple_of(start, 16), size)
                down_ref[rows, :] = ref[:size, :]
                tgate_ref[rows, :] = ref[size:2 * size, :]
                tup_ref[rows, :] = ref[2 * size:, :]
            start = ((at_ref[0] + 2) % 4) * FS + at
            rows = pl.ds(pl.multiple_of(start, 16), size)
            down_ref[rows, :] = far_a[:size, :]
            tgate_ref[pl.ds(pl.multiple_of(start, 16), half - size), :] = far_a[size:, :]
            tgate_ref[pl.ds(pl.multiple_of(start + half - size, 16), 2 * size - half), :] = far_b[:2 * size - half, :]
            tup_ref[rows, :] = far_b[2 * size - half:, :]

        def turn(i, carry):
            cut = pl.ds(pl.multiple_of(i * 128, 128), 128)
            gate_ref[:, cut] = tgate_ref[cut, :].T
            up_ref[:, cut] = tup_ref[cut, :].T
            return carry

        lax.fori_loop(0, 14, turn, 0)

    args = [a for g in groups for a in g[2]]
    outs = [sds((512, 4 * FS), BF), sds((512, 4 * FS), BF), sds((4 * FS, 512), BF)]
    scratch = [pltpu.VMEM((4 * FS, 512), BF), pltpu.VMEM((4 * FS, 512), BF)]
    return call(kernel, outs, (depth_at,), *args, scratch=scratch, hbm_out=(0, 1, 2), limit=24)


def step(tokens, norm_gain, w_gate, w_up, w_down, cotangent):
    x_at = jnp.reshape(lax.axis_index("row") // 2, (1,)).astype(jnp.int32)
    depth_at = jnp.reshape(lax.axis_index("depth"), (1,)).astype(jnp.int32)
    gain = norm_gain[None, :]
    count = len(CHUNKS)

    both = pack_call(tokens, cotangent)
    both = join_call([both] + [send_zl(both, k) for k in (1, 2, 3)])
    near = [send_y(both, k) for k in (1, -1, 2)]
    weights = prepare_call(depth_at, w_gate, w_up, w_down)
    both = join_call([both] + near)
    both = join_call([both, send_core(both)])
    chunks = [(at, size, weights[2 * i], weights[2 * i + 1]) for i, (at, size) in enumerate(CHUNKS)]

    received = []
    for n, (at, size, wgu, wd) in enumerate(chunks):
        groups = [(2,), (1,), (-1,)] if n == 0 else [(2, 1, -1)]
        arrived = []
        for ks in groups:
            parts = partial_call(x_at, ks, both, gain, wgu, wd, size, n == 0)
            arrived += [send_x(part, k) for k, part in zip(ks, parts)]
        received.append(arrived)
    halves = []
    for n, (at, size, wgu, wd) in enumerate(chunks):
        total, message = sum_call(x_at, both, gain, wgu, wd, received[n], size, n == 0)
        halves.append((total, send_zh(message)))
    pieces = []
    grads = []

    def middle(n, inv):
        _, size, _, _ = chunks[n]
        mine, inv = middle_call(*halves[n], inv, size)
        pieces.append([mine] + [send_x(mine, k) for k in (2, 1, -1)])
        return inv

    def weight_grad(n):
        at, size, _, _ = chunks[n]
        grad = weight_grad_call(x_at, pieces[n], both, gain, size)
        grads.append((at, size, grad, send_y(grad, 1), send_y(grad, -1)))

    def relay(n):
        at, size, grad, prev, after = grads[n]
        half = 3 * size // 2
        return at, size, [grad, prev, after, send_y(prev[:half], 1), send_y(after[half:], -1)]

    def back(n, before):
        _, size, wgu, wd = chunks[n]
        return back_call(x_at, pieces[n], wgu, wd, before, both, size, n == count - 1)

    inv = middle(0, None)
    weight_grad(0)
    middle(1, inv)
    *before, inv = back(0, None)
    groups = [relay(0)]
    own, gain_part, inner, message = back(1, before)
    message = send_core(message)
    weight_grad(1)
    strips = [[(128 * a + 32 * j, 32) for a in range(4)] for j in range(4)]
    own, gain_part, inner, *messages = fold_call(own, gain_part, inner, [message], [0], strips)
    messages = [send_zl(m, -k) for k, m in zip((1, 2, 3), messages)]
    groups.append(relay(1))
    strips = [[(32 * j, 32)] for j in range(4)]
    own, gain_part, inner, *messages = fold_call(own, gain_part, inner, messages, [32, 64, 96], strips)
    messages = [send_y(m, k) for k, m in zip((-1, 1, 2), messages)]
    output, grad_tokens, gain_grad = final_call(own, gain_part, inner, inv, messages, tokens, cotangent, gain)
    out_gate, out_up, out_down = assemble_call(depth_at, groups)
    return output, grad_tokens, gain_grad[0], out_gate, out_up, out_down


def solution(mesh):
    in_specs = (
        P(("col", "depth"), "row"),
        P("row"),
        P("row", "col"),
        P("row", "col"),
        P("col", "row"),
        P(("col", "depth"), "row"),
    )
    out_specs = (
        P(("col", "depth"), "row"),
        P(("col", "depth"), "row"),
        P("row"),
        P("row", "col"),
        P("row", "col"),
        P("col", "row"),
    )
    function = jax.shard_map(step, mesh=mesh, in_specs=in_specs, out_specs=out_specs, check_vma=False)
    shapes = [((1024, D), BF), ((D,), F32), ((D, 32 * FS), BF), ((D, 32 * FS), BF), ((32 * FS, D), BF), ((1024, D), BF)]
    jax.eval_shape(function, *[sds(*shape) for shape in shapes])
    return function
```

```python
import jax
import jax.numpy as jnp
from jax import lax
from jax.experimental import pallas as pl
from jax.experimental.pallas import tpu as pltpu
from jax.sharding import PartitionSpec as P


D = 4096
EPS = 1e-05
FS = 448
CHUNKS = ((0, 128), (128, 160), (288, 160))


BF = jnp.bfloat16
F32 = jnp.float32


def perm_x(k):
    return [(r, ((r // 2 + k) % 4) * 2 + r % 2) for r in range(8)]


PERM_ZH = [(r, r ^ 1) for r in range(8)]


def perm_zl(k):
    return [(c, c ^ (2 * k)) for c in range(8)]


PERM_CORE = [(c, c ^ 1) for c in range(8)]


def perm_y(k):
    return [(d, d ^ k) for d in range(4)]


def send(v, axis, perm):
    return lax.ppermute(v, axis, perm)


def send_x(v, k):
    return send(v, "row", perm_x(k))


def send_zh(v):
    return send(v, "row", PERM_ZH)


def send_zl(v, k):
    return send(v, "col", perm_zl(k))


def send_core(v):
    return send(v, "col", PERM_CORE)


def send_y(v, k):
    return send(v, "depth", perm_y(k))


def nt(left, right):
    return lax.dot_general(left, right, (((1,), (1,)), ((), ())), preferred_element_type=F32)


def nn(left, right):
    return lax.dot_general(left, right, (((1,), (0,)), ((), ())), preferred_element_type=F32)


def tn(left, right):
    return lax.dot_general(left, right, (((0,), (0,)), ((), ())), preferred_element_type=F32)


VM = pl.BlockSpec(memory_space=pltpu.VMEM)
SM = pl.BlockSpec(memory_space=pltpu.SMEM)


def sds(shape, dtype):
    return jax.ShapeDtypeStruct(shape, dtype)


ANY = pl.BlockSpec(memory_space=pl.ANY)


def call(kernel, outs, scalars, *args, scratch=(), raw=0, hbm_in=(), hbm_out=(), limit=12):
    outs = [o if i in hbm_out else pltpu.VMEM(o.shape, o.dtype) for i, o in enumerate(outs)]
    run = pl.pallas_call(
        kernel,
        out_shape=outs,
        in_specs=[SM] * len(scalars) + [ANY] * raw + [VM] * (len(args) - raw),
        out_specs=[VM] * len(outs),
        scratch_shapes=list(scratch),
        compiler_params=pltpu.CompilerParams(vmem_limit_bytes=limit << 20),
    )
    placed = [
        pltpu.with_memory_space_constraint(a, pltpu.HBM if i < raw or i in hbm_in else pltpu.VMEM)
        for i, a in enumerate(args)
    ]
    return run(*scalars, *placed)


def split(value):
    hi = value.astype(BF)
    return hi, (value - hi.astype(F32)).astype(BF)


def add_stat(message, size):
    return message[3 * size:3 * size + 8, :].astype(F32) + message[3 * size + 8:, :].astype(F32)


def pack_call(tokens, cotangent):
    def kernel(tok_ref, cot_ref, out_ref):
        out_ref[:, :512] = tok_ref[...]
        out_ref[:, 512:] = cot_ref[...]

    return call(kernel, [sds((32, 1024), BF)], (), tokens, cotangent, hbm_in=(0, 1))[0]


def join_call(parts):
    rows = parts[0].shape[0]

    def kernel(*refs):
        for i, ref in enumerate(refs[:-1]):
            refs[-1][rows * i:rows * (i + 1), :] = ref[...]

    return call(kernel, [sds((rows * len(parts), 1024), BF)], (), *parts)[0]


def prepare_call(depth_at, w_gate, w_up, w_down):
    def kernel(at_ref, gate_ref, up_ref, down_ref, *refs):
        outs, (cut_ref, turned_ref, sems) = refs[:-3], refs[-3:]
        at = at_ref[0]
        start = pl.multiple_of(((7 * at) // 2) * 128, 128)
        skip = pl.multiple_of((at % 2) * 64, 64)
        copies = [
            pltpu.make_async_copy(ref.at[:, pl.ds(start, 512)], cut_ref.at[i], sems.at[i])
            for i, ref in enumerate((gate_ref, up_ref))
        ]
        for i, (where, size) in enumerate(CHUNKS):
            rows = pl.ds(pl.multiple_of(at * FS + where, 16), size)
            copies.append(pltpu.make_async_copy(down_ref.at[rows, :], outs[2 * i + 1], sems.at[2 + i]))
        for copy in copies:
            copy.start()
        for which in (0, 1):
            copies[which].wait()
            turned_ref[which] = cut_ref[which].T
            for i, (where, size) in enumerate(CHUNKS):
                outs[2 * i][which * size:(which + 1) * size, :] = turned_ref[which, pl.ds(skip + where, size), :]
        for copy in copies[2:]:
            copy.wait()

    outs = []
    for _, size in CHUNKS:
        outs += [sds((2 * size, 512), BF), sds((size, 512), BF)]
    scratch = [pltpu.VMEM((2, 512, 512), BF), pltpu.VMEM((2, 512, 512), BF), pltpu.SemaphoreType.DMA((2 + len(CHUNKS),))]
    return call(kernel, outs, (depth_at,), w_gate, w_up, w_down, scratch=scratch, raw=3)


def block_rows(at_ref, k):
    return pl.ds(pl.multiple_of(((at_ref[0] + k + 4) % 4) * 256, 256), 256)


def block_part(rows, both_ref, gain_ref, wgu_ref, wd_ref, first):
    x = both_ref[rows, :512].astype(F32)
    parts = [nt(wgu_ref[...], (x * gain_ref[...]).astype(BF)), nt(wd_ref[...], both_ref[rows, 512:])]
    if first:
        hi, lo = split(x * x)
        ones = jnp.ones((8, 512), BF)
        parts.append(nt(ones, hi) + nt(ones, lo))
    return parts


def write_parts(ref, parts, size):
    ref[:2 * size, :] = parts[0].astype(BF)
    ref[2 * size:3 * size, :] = parts[1].astype(BF)
    if len(parts) > 2:
        hi, lo = split(parts[2])
        ref[3 * size:, :] = jnp.concatenate([hi, lo], axis=0)


def read_parts(ref, size, first):
    parts = [ref[:2 * size, :].astype(F32), ref[2 * size:3 * size, :].astype(F32)]
    if first:
        parts.append(add_stat(ref, size))
    return parts


def message_shape(size, first):
    return sds((3 * size + (16 if first else 0), 256), BF)


def partial_call(x_at, ks, both, gain, wgu, wd, size, first):
    def kernel(at_ref, both_ref, gain_ref, wgu_ref, wd_ref, *outs):
        for k, out_ref in zip(ks, outs):
            write_parts(out_ref, block_part(block_rows(at_ref, k), both_ref, gain_ref, wgu_ref, wd_ref, first), size)

    return call(kernel, [message_shape(size, first)] * len(ks), (x_at,), both, gain, wgu, wd)


def sum_call(x_at, both, gain, wgu, wd, received, size, first):
    def kernel(at_ref, both_ref, gain_ref, wgu_ref, wd_ref, a_ref, b_ref, c_ref, total_ref, out_ref):
        total = block_part(block_rows(at_ref, 0), both_ref, gain_ref, wgu_ref, wd_ref, first)
        for ref in (a_ref, b_ref, c_ref):
            total = [a + b for a, b in zip(total, read_parts(ref, size, first))]
        total_ref[:2 * size, :] = total[0]
        total_ref[2 * size:3 * size, :] = total[1]
        if first:
            total_ref[3 * size:, :] = total[2]
        write_parts(out_ref, total, size)

    outs = [sds((3 * size + (8 if first else 0), 256), F32), message_shape(size, first)]
    return call(kernel, outs, (x_at,), both, gain, wgu, wd, *received)


def middle_call(total, other, inv, size):
    first = inv is None

    def kernel(total_ref, other_ref, *refs):
        if first:
            out_ref, inv_ref = refs
            stat = total_ref[3 * size:, :] + add_stat(other_ref, size)
            inv_ref[...] = lax.rsqrt(stat / D + EPS)
        else:
            inv_ref, out_ref = refs
        scale = inv_ref[0:1, :]
        gate = (total_ref[:size, :] + other_ref[:size, :].astype(F32)) * scale
        up = (total_ref[size:2 * size, :] + other_ref[size:2 * size, :].astype(F32)) * scale
        grad = (total_ref[2 * size:3 * size, :] + other_ref[2 * size:3 * size, :].astype(F32)) * scale
        sig = jax.nn.sigmoid(gate)
        act = gate * sig
        out_ref[:size, :] = (act * up).astype(BF)
        grad_gate = grad * up * sig * (1.0 + gate * (1.0 - sig))
        grad_up = grad * act
        out_ref[size:2 * size, :] = grad_gate.astype(BF)
        out_ref[2 * size:3 * size, :] = grad_up.astype(BF)
        inner = jnp.sum(grad_gate * gate + grad_up * up, axis=0, keepdims=True)
        hi, lo = split(jnp.broadcast_to(inner, (8, 256)))
        out_ref[3 * size:3 * size + 16, :] = jnp.concatenate([hi, lo], axis=0)
        if first:
            hi, lo = split(inv_ref[...])
            out_ref[3 * size + 16:, :] = jnp.concatenate([hi, lo], axis=0)

    out = sds((3 * size + (32 if first else 16), 256), BF)
    if first:
        return call(kernel, [out, sds((8, 256), F32)], (), total, other)
    return call(kernel, [out], (), total, other, inv)[0], inv


def weight_grad_call(x_at, groups, sizes, both, gain):
    def kernel(at_ref, *refs):
        both_ref, gain_ref, out_ref = refs[-3:]
        to = 0
        for i, size in enumerate(sizes):
            down = jnp.zeros((size, 512), F32)
            gate_up = jnp.zeros((2 * size, 512), F32)
            for k, ref in zip((0, 2, 1, -1), refs[4 * i:4 * i + 4]):
                rows = block_rows(at_ref, -k)
                u = (both_ref[rows, :512].astype(F32) * gain_ref[...]).astype(BF)
                down = down + nn(ref[:size, :], both_ref[rows, 512:])
                gate_up = gate_up + nn(ref[size:3 * size, :], u)
            out_ref[to:to + size, :] = down.astype(BF)
            out_ref[to + size:to + 3 * size, :] = gate_up.astype(BF)
            to += 3 * size

    pieces = [piece for group in groups for piece in group]
    return call(kernel, [sds((3 * sum(sizes), 512), BF)], (x_at,), *pieces, both, gain)[0]


def write_extra(ref, rows, gain_part, inner):
    gain_hi, gain_lo = split(gain_part)
    inner_hi, inner_lo = split(inner)
    ref[rows:, :512] = jnp.concatenate([gain_hi, inner_hi], axis=0)
    ref[rows:, 512:] = jnp.concatenate([gain_lo, inner_lo], axis=0)


def read_extra(ref, rows):
    extra = ref[rows:, :].astype(F32)
    extra = extra[:, :512] + extra[:, 512:]
    return extra[:8, :], extra[8:, :]


def read_pair(ref, at):
    return ref[at:at + 8, :].astype(F32) + ref[at + 8:at + 16, :].astype(F32)


def back_call(x_at, pieces, wgu, wd, before, both, size, last):
    first = before is None

    def kernel(at_ref, a_ref, b_ref, c_ref, d_ref, wgu_ref, wd_ref, both_ref, *refs):
        refs = list(refs)
        if not first:
            before_ref, before_inner_ref = refs.pop(0), refs.pop(0)
        if last:
            own_ref, gain_ref, own_inner_ref, out_ref, acc_ref, inner_ref = refs
        elif first:
            acc_ref, inner_ref, inv_ref, all_inv_ref = refs
        else:
            acc_ref, inner_ref = refs
        gain_part = jnp.zeros((1, 512), F32)
        for k, ref in zip((0, 2, 1, -1), (a_ref, b_ref, c_ref, d_ref)):
            rows = block_rows(at_ref, -k)
            mixed = tn(ref[:size, :], wd_ref[...])
            grad = tn(ref[size:3 * size, :], wgu_ref[...])
            inner = read_pair(ref, 3 * size)
            if not first:
                mixed = mixed + before_ref[rows, :512]
                grad = grad + before_ref[rows, 512:]
                inner = inner + before_inner_ref[:, rows]
            acc_ref[rows, :512] = mixed
            acc_ref[rows, 512:] = grad
            inner_ref[:, rows] = inner
            if first:
                all_inv_ref[:, rows] = read_pair(ref, 3 * size + 16)
            if last:
                gain_part = gain_part + jnp.sum(grad * both_ref[rows, :512].astype(F32), axis=0, keepdims=True)
        if first:
            inv_ref[...] = all_inv_ref[:, :128]
        if last:
            own_ref[...] = acc_ref[:512, :]
            own_inner_ref[...] = inner_ref[:, :512]
            out_ref[:512, :] = acc_ref[512:, :].astype(BF)
            gain_part = jnp.broadcast_to(gain_part, (8, 512))
            gain_ref[...] = gain_part
            write_extra(out_ref, 512, gain_part, inner_ref[:, 512:])

    args = list(pieces) + [wgu, wd, both] + ([] if first else list(before))
    acc, inner = sds((1024, 1024), F32), sds((8, 1024), F32)
    if last:
        outs = [sds((512, 1024), F32), sds((8, 512), F32), sds((8, 512), F32), sds((528, 1024), BF)]
        scratch = [pltpu.VMEM(acc.shape, F32), pltpu.VMEM(inner.shape, F32)]
        return call(kernel, outs, (x_at,), *args, scratch=scratch)
    if first:
        return call(kernel, [acc, inner, sds((8, 128), F32)], (x_at,), *args, scratch=[pltpu.VMEM((8, 1024), F32)])
    return call(kernel, [acc, inner], (x_at,), *args)


def turn_left(inner, lanes):
    return jnp.concatenate(
        [pltpu.roll(inner[:, 128 * i:128 * (i + 1)], 128 - lanes, 1) for i in range(4)], axis=1)


def upper_half(inner):
    return jnp.concatenate([inner[:, 256:], inner[:, 256:]], axis=1)


def fold_call(own, gain_part, inner, messages, turns, strips):
    rows = own.shape[0]
    count = len(messages)
    keep = sum(size for _, size in strips[0])

    def kernel(own_ref, gain_ref, inner_ref, *refs):
        received = refs[:count]
        keep_ref, gain_out_ref, inner_out_ref = refs[count:count + 3]
        outs = refs[count + 3:]
        gain_sum, inner_sum = gain_ref[...], inner_ref[...]
        for ref, turn in zip(received, turns):
            gain_more, inner_more = read_extra(ref, rows)
            gain_sum = gain_sum + gain_more
            inner_sum = inner_sum + (turn(inner_more) if turn else inner_more)
        gain_out_ref[...] = gain_sum
        inner_out_ref[...] = inner_sum
        for strip, out in zip(strips, (keep_ref,) + tuple(outs)):
            to = 0
            for at, size in strip:
                total = own_ref[at:at + size, :]
                for ref in received:
                    total = total + ref[at:at + size, :].astype(F32)
                out[to:to + size, :] = total.astype(out.dtype)
                to += size
        for ref in outs:
            write_extra(ref, keep, gain_sum, inner_sum)

    outs = [sds((keep, 1024), F32), sds((8, 512), F32), sds((8, 512), F32)]
    outs += [sds((keep + 16, 1024), BF)] * (len(strips) - 1)
    return call(kernel, outs, (), own, gain_part, inner, *messages)


def as_column(rows):
    hi, lo = split(rows)
    eighth = jnp.full((16, 128), 0.125, BF)
    return tn(jnp.concatenate([hi, lo], axis=0), eighth)[:32, :1]


def final_call(own, gain_part, inner, inv, message, tokens, cotangent, gain):
    def kernel(own_ref, part_ref, inner_ref, inv_ref, a_ref, tok_ref, cot_ref, gain_ref, out_ref, grad_ref, vec_ref):
        total = own_ref[...] + a_ref[:32, :].astype(F32)
        gain_more, inner_more = read_extra(a_ref, 32)
        gain_sum = part_ref[...] + gain_more
        inner_sum = inner_ref[:, :128] + inner_more[:, 128:256]
        vec_ref[...] = gain_sum[:1, :]
        x = tok_ref[...].astype(F32)
        out_ref[...] = (x + total[:, :512]).astype(BF)
        scale = as_column(inv_ref[...]) * (as_column(inner_sum) / D)
        grad_ref[...] = (cot_ref[...].astype(F32) + total[:, 512:] * gain_ref[...] - x * scale).astype(BF)

    outs = [sds((32, 512), BF), sds((32, 512), BF), sds((1, 512), F32)]
    return call(kernel, outs, (), own, gain_part, inner, inv, message, tokens, cotangent, gain, hbm_out=(0, 1, 2))


def assemble_call(depth_at, groups):
    counts = [sum(len(pieces) for _, pieces in arrived) for _, arrived in groups]

    def kernel(at_ref, *refs):
        gate_ref, up_ref, down_ref, tgate_ref, tup_ref = refs[sum(counts):]
        refs = list(refs[:sum(counts)])
        for chunks, arrived in groups:
            segments = []
            for at, size in chunks:
                segments += [(ref, at, size) for ref in (down_ref, tgate_ref, tup_ref)]
            for source, pieces in arrived:
                base = (at_ref[0] ^ source) * FS
                todo = list(segments)
                for piece in pieces:
                    ref, to = refs.pop(0), 0
                    while to < piece.shape[0]:
                        target, at, size = todo.pop(0)
                        take = min(size, piece.shape[0] - to)
                        target[pl.ds(pl.multiple_of(base + at, 16), take), :] = ref[to:to + take, :]
                        to += take
                        if take < size:
                            todo.insert(0, (target, at + take, size - take))

        def turn(i, carry):
            cut = pl.ds(pl.multiple_of(i * 128, 128), 128)
            gate_ref[:, cut] = tgate_ref[cut, :].T
            up_ref[:, cut] = tup_ref[cut, :].T
            return carry

        lax.fori_loop(0, 14, turn, 0)

    args = [piece for _, arrived in groups for _, pieces in arrived for piece in pieces]
    outs = [sds((512, 4 * FS), BF), sds((512, 4 * FS), BF), sds((4 * FS, 512), BF)]
    scratch = [pltpu.VMEM((4 * FS, 512), BF), pltpu.VMEM((4 * FS, 512), BF)]
    return call(kernel, outs, (depth_at,), *args, scratch=scratch, hbm_out=(0, 1, 2), limit=24)


def step(tokens, norm_gain, w_gate, w_up, w_down, cotangent):
    x_at = jnp.reshape(lax.axis_index("row") // 2, (1,)).astype(jnp.int32)
    depth_at = jnp.reshape(lax.axis_index("depth"), (1,)).astype(jnp.int32)
    gain = norm_gain[None, :]
    count = len(CHUNKS)

    both = pack_call(tokens, cotangent)
    both = join_call([both, send_zl(both, 1)])
    both = join_call([both, send_zl(both, 2)])
    near = [send_y(both, k) for k in (1, 2, 3)]
    weights = prepare_call(depth_at, w_gate, w_up, w_down)
    both = join_call([both] + near)
    both = join_call([both, send_core(both)])
    chunks = [(at, size, weights[2 * i], weights[2 * i + 1]) for i, (at, size) in enumerate(CHUNKS)]

    received = []

    def partials(n):
        _, size, wgu, wd = chunks[n]
        arrived = []
        for ks in [(2,), (1,), (-1,)] if n == 0 else [(2, 1, -1)]:
            parts = partial_call(x_at, ks, both, gain, wgu, wd, size, n == 0)
            arrived += [send_x(part, k) for k, part in zip(ks, parts)]
        received.append(arrived)

    halves = []

    def row_sum(n):
        _, size, wgu, wd = chunks[n]
        total, message = sum_call(x_at, both, gain, wgu, wd, received[n], size, n == 0)
        halves.append((total, send_zh(message)))

    pieces = []

    def middle(n, inv):
        _, size, _, _ = chunks[n]
        mine, inv = middle_call(*halves[n], inv, size)
        pieces.append([mine] + [send_x(mine, k) for k in (2, 1, -1)])
        return inv

    def weight_grad(ns):
        grad = weight_grad_call(
            x_at, [pieces[n] for n in ns], [CHUNKS[n][1] for n in ns], both, gain)
        arrived = [(0, [grad])]
        return [CHUNKS[n] for n in ns], arrived

    def spread(group, ks):
        for k in ks:
            group[1].append((k, [send_y(group[1][0][1][0], k)]))

    def relay(group):
        near = {source: pieces[0] for source, pieces in group[1]}
        half = near[0].shape[0] // 2
        group[1].append((2, [send_y(near[1][:half], 3), send_y(near[3][half:], 1)]))

    def back(n, before):
        _, size, wgu, wd = chunks[n]
        return back_call(x_at, pieces[n], wgu, wd, before, both, size, n == count - 1)

    partials(0)
    partials(1)
    row_sum(0)
    partials(2)
    row_sum(1)
    inv = middle(0, None)
    row_sum(2)
    middle(1, inv)
    *before, own_inv = back(0, None)
    middle(2, inv)
    early = weight_grad((0, 1))
    spread(early, (1, 3))
    before = back(1, before)
    own, gain_part, inner, message = back(2, before)
    message = send_core(message)
    late = weight_grad((2,))
    strips = [[(128 * a + 32 * j, 32) for a in range(4)] for j in range(4)]
    own, gain_part, inner, *messages = fold_call(own, gain_part, inner, [message], [None], strips)
    messages = [send_zl(m, k) for k, m in zip((1, 2, 3), messages)]
    relay(early)
    spread(late, (1, 3, 2))
    turns = [lambda v, lanes=lanes: turn_left(v, lanes) for lanes in (32, 64, 96)]
    own, gain_part, inner, *messages = fold_call(
        own, gain_part, inner, messages, turns, [[(0, 64)], [(64, 64)]])
    message = send_y(messages[0], 2)
    own, gain_part, inner, *messages = fold_call(
        own, gain_part, inner, [message], [upper_half], [[(0, 32)], [(32, 32)]])
    message = send_y(messages[0], 1)
    out_gate, out_up, out_down = assemble_call(depth_at, [early, late])
    output, grad_tokens, gain_grad = final_call(own, gain_part, inner, own_inv, message, tokens, cotangent, gain)
    return output, grad_tokens, gain_grad[0], out_gate, out_up, out_down


def solution(mesh):
    in_specs = (
        P(("col", "depth"), "row"),
        P("row"),
        P("row", "col"),
        P("row", "col"),
        P("col", "row"),
        P(("col", "depth"), "row"),
    )
    out_specs = (
        P(("col", "depth"), "row"),
        P(("col", "depth"), "row"),
        P("row"),
        P("row", "col"),
        P("row", "col"),
        P("col", "row"),
    )
    function = jax.shard_map(step, mesh=mesh, in_specs=in_specs, out_specs=out_specs, check_vma=False)
    shapes = [((1024, D), BF), ((D,), F32), ((D, 32 * FS), BF), ((D, 32 * FS), BF), ((32 * FS, D), BF), ((1024, D), BF)]
    jax.eval_shape(function, *[sds(*shape) for shape in shapes])
    return function
```

```python
import jax
import jax.numpy as jnp
from jax import lax
from jax.experimental import pallas as pl
from jax.experimental.pallas import tpu as pltpu
from jax.sharding import PartitionSpec as P


D = 4096
EPS = 1e-05
FS = 448
CHUNKS = ((0, 128), (128, 160), (288, 160))


BF = jnp.bfloat16
F32 = jnp.float32


def perm_x(k):
    return [(r, ((r // 2 + k) % 4) * 2 + r % 2) for r in range(8)]


PERM_ZH = [(r, r ^ 1) for r in range(8)]


def perm_zl(k):
    return [(c, c ^ (2 * k)) for c in range(8)]


PERM_CORE = [(c, c ^ 1) for c in range(8)]


def perm_y(k):
    return [(d, d ^ k) for d in range(4)]


def send(v, axis, perm):
    return lax.ppermute(v, axis, perm)


def send_x(v, k):
    return send(v, "row", perm_x(k))


def send_zh(v):
    return send(v, "row", PERM_ZH)


def send_zl(v, k):
    return send(v, "col", perm_zl(k))


def send_core(v):
    return send(v, "col", PERM_CORE)


def send_y(v, k):
    return send(v, "depth", perm_y(k))


def nt(left, right):
    return lax.dot_general(left, right, (((1,), (1,)), ((), ())), preferred_element_type=F32)


def nn(left, right):
    return lax.dot_general(left, right, (((1,), (0,)), ((), ())), preferred_element_type=F32)


def tn(left, right):
    return lax.dot_general(left, right, (((0,), (0,)), ((), ())), preferred_element_type=F32)


VM = pl.BlockSpec(memory_space=pltpu.VMEM)
SM = pl.BlockSpec(memory_space=pltpu.SMEM)


def sds(shape, dtype):
    return jax.ShapeDtypeStruct(shape, dtype)


ANY = pl.BlockSpec(memory_space=pl.ANY)


def call(kernel, outs, scalars, *args, scratch=(), raw=0, hbm_in=(), hbm_out=(), limit=12):
    outs = [o if i in hbm_out else pltpu.VMEM(o.shape, o.dtype) for i, o in enumerate(outs)]
    run = pl.pallas_call(
        kernel,
        out_shape=outs,
        in_specs=[SM] * len(scalars) + [ANY] * raw + [VM] * (len(args) - raw),
        out_specs=[VM] * len(outs),
        scratch_shapes=list(scratch),
        compiler_params=pltpu.CompilerParams(vmem_limit_bytes=limit << 20),
    )
    placed = [
        pltpu.with_memory_space_constraint(a, pltpu.HBM if i < raw or i in hbm_in else pltpu.VMEM)
        for i, a in enumerate(args)
    ]
    return run(*scalars, *placed)


def split(value):
    hi = value.astype(BF)
    return hi, (value - hi.astype(F32)).astype(BF)


def add_stat(message, size):
    return message[3 * size:3 * size + 8, :].astype(F32) + message[3 * size + 8:, :].astype(F32)


def pack_call(tokens, cotangent):
    def kernel(tok_ref, cot_ref, out_ref):
        out_ref[:, :512] = tok_ref[...]
        out_ref[:, 512:] = cot_ref[...]

    return call(kernel, [sds((32, 1024), BF)], (), tokens, cotangent, hbm_in=(0, 1))[0]


def join_call(parts):
    rows = parts[0].shape[0]

    def kernel(*refs):
        for i, ref in enumerate(refs[:-1]):
            refs[-1][rows * i:rows * (i + 1), :] = ref[...]

    return call(kernel, [sds((rows * len(parts), 1024), BF)], (), *parts)[0]


def prepare_call(depth_at, w_gate, w_up, w_down):
    def kernel(at_ref, gate_ref, up_ref, down_ref, *refs):
        outs, (cut_ref, turned_ref, sems) = refs[:-3], refs[-3:]
        at = at_ref[0]
        start = pl.multiple_of(((7 * at) // 2) * 128, 128)
        skip = pl.multiple_of((at % 2) * 64, 64)
        copies = [
            pltpu.make_async_copy(ref.at[:, pl.ds(start, 512)], cut_ref.at[i], sems.at[i])
            for i, ref in enumerate((gate_ref, up_ref))
        ]
        for i, (where, size) in enumerate(CHUNKS):
            rows = pl.ds(pl.multiple_of(at * FS + where, 16), size)
            copies.append(pltpu.make_async_copy(down_ref.at[rows, :], outs[2 * i + 1], sems.at[2 + i]))
        for copy in copies:
            copy.start()
        for which in (0, 1):
            copies[which].wait()
            turned_ref[which] = cut_ref[which].T
            for i, (where, size) in enumerate(CHUNKS):
                outs[2 * i][which * size:(which + 1) * size, :] = turned_ref[which, pl.ds(skip + where, size), :]
        for copy in copies[2:]:
            copy.wait()

    outs = []
    for _, size in CHUNKS:
        outs += [sds((2 * size, 512), BF), sds((size, 512), BF)]
    scratch = [pltpu.VMEM((2, 512, 512), BF), pltpu.VMEM((2, 512, 512), BF), pltpu.SemaphoreType.DMA((2 + len(CHUNKS),))]
    return call(kernel, outs, (depth_at,), w_gate, w_up, w_down, scratch=scratch, raw=3)


def block_rows(at_ref, k):
    return pl.ds(pl.multiple_of(((at_ref[0] + k + 4) % 4) * 256, 256), 256)


def block_part(rows, both_ref, gain_ref, wgu_ref, wd_ref, first):
    x = both_ref[rows, :512].astype(F32)
    parts = [nt(wgu_ref[...], (x * gain_ref[...]).astype(BF)), nt(wd_ref[...], both_ref[rows, 512:])]
    if first:
        hi, lo = split(x * x)
        ones = jnp.ones((8, 512), BF)
        parts.append(nt(ones, hi) + nt(ones, lo))
    return parts


def write_parts(ref, parts, size):
    ref[:2 * size, :] = parts[0].astype(BF)
    ref[2 * size:3 * size, :] = parts[1].astype(BF)
    if len(parts) > 2:
        hi, lo = split(parts[2])
        ref[3 * size:, :] = jnp.concatenate([hi, lo], axis=0)


def read_parts(ref, size, first):
    parts = [ref[:2 * size, :].astype(F32), ref[2 * size:3 * size, :].astype(F32)]
    if first:
        parts.append(add_stat(ref, size))
    return parts


def message_shape(size, first):
    return sds((3 * size + (16 if first else 0), 256), BF)


def partial_call(x_at, ks, both, gain, wgu, wd, size, first):
    def kernel(at_ref, both_ref, gain_ref, wgu_ref, wd_ref, *outs):
        for k, out_ref in zip(ks, outs):
            write_parts(out_ref, block_part(block_rows(at_ref, k), both_ref, gain_ref, wgu_ref, wd_ref, first), size)

    return call(kernel, [message_shape(size, first)] * len(ks), (x_at,), both, gain, wgu, wd)


def sum_call(x_at, both, gain, wgu, wd, received, size, first):
    def kernel(at_ref, both_ref, gain_ref, wgu_ref, wd_ref, a_ref, b_ref, c_ref, total_ref, out_ref):
        total = block_part(block_rows(at_ref, 0), both_ref, gain_ref, wgu_ref, wd_ref, first)
        for ref in (a_ref, b_ref, c_ref):
            total = [a + b for a, b in zip(total, read_parts(ref, size, first))]
        total_ref[:2 * size, :] = total[0]
        total_ref[2 * size:3 * size, :] = total[1]
        if first:
            total_ref[3 * size:, :] = total[2]
        write_parts(out_ref, total, size)

    outs = [sds((3 * size + (8 if first else 0), 256), F32), message_shape(size, first)]
    return call(kernel, outs, (x_at,), both, gain, wgu, wd, *received)


def middle_call(total, other, inv, size):
    first = inv is None

    def kernel(total_ref, other_ref, *refs):
        if first:
            out_ref, inv_ref = refs
            stat = total_ref[3 * size:, :] + add_stat(other_ref, size)
            inv_ref[...] = lax.rsqrt(stat / D + EPS)
        else:
            inv_ref, out_ref = refs
        scale = inv_ref[0:1, :]
        gate = (total_ref[:size, :] + other_ref[:size, :].astype(F32)) * scale
        up = (total_ref[size:2 * size, :] + other_ref[size:2 * size, :].astype(F32)) * scale
        grad = (total_ref[2 * size:3 * size, :] + other_ref[2 * size:3 * size, :].astype(F32)) * scale
        sig = jax.nn.sigmoid(gate)
        act = gate * sig
        out_ref[:size, :] = (act * up).astype(BF)
        grad_gate = grad * up * sig * (1.0 + gate * (1.0 - sig))
        grad_up = grad * act
        out_ref[size:2 * size, :] = grad_gate.astype(BF)
        out_ref[2 * size:3 * size, :] = grad_up.astype(BF)
        inner = jnp.sum(grad_gate * gate + grad_up * up, axis=0, keepdims=True)
        hi, lo = split(jnp.broadcast_to(inner, (8, 256)))
        out_ref[3 * size:3 * size + 16, :] = jnp.concatenate([hi, lo], axis=0)
        if first:
            hi, lo = split(inv_ref[...])
            out_ref[3 * size + 16:, :] = jnp.concatenate([hi, lo], axis=0)

    out = sds((3 * size + (32 if first else 16), 256), BF)
    if first:
        return call(kernel, [out, sds((8, 256), F32)], (), total, other)
    return call(kernel, [out], (), total, other, inv)[0], inv


def weight_grad_call(x_at, groups, sizes, both, gain):
    def kernel(at_ref, *refs):
        both_ref, gain_ref, out_ref = refs[-3:]
        to = 0
        for i, size in enumerate(sizes):
            down = jnp.zeros((size, 512), F32)
            gate_up = jnp.zeros((2 * size, 512), F32)
            for k, ref in zip((0, 2, 1, -1), refs[4 * i:4 * i + 4]):
                rows = block_rows(at_ref, -k)
                u = (both_ref[rows, :512].astype(F32) * gain_ref[...]).astype(BF)
                down = down + nn(ref[:size, :], both_ref[rows, 512:])
                gate_up = gate_up + nn(ref[size:3 * size, :], u)
            out_ref[to:to + size, :] = down.astype(BF)
            out_ref[to + size:to + 3 * size, :] = gate_up.astype(BF)
            to += 3 * size

    pieces = [piece for group in groups for piece in group]
    return call(kernel, [sds((3 * sum(sizes), 512), BF)], (x_at,), *pieces, both, gain)[0]


def write_extra(ref, rows, gain_part, inner):
    upper = lax.broadcasted_iota(jnp.int32, (8, 512), 0) < 4
    hi, lo = split(jnp.where(upper, gain_part, inner))
    ref[rows:, :512] = hi
    ref[rows:, 512:] = lo


def read_extra(ref, rows):
    extra = ref[rows:, :].astype(F32)
    extra = extra[:, :512] + extra[:, 512:]
    return jnp.broadcast_to(extra[:1, :], (8, 512)), jnp.broadcast_to(extra[4:5, :], (8, 512))


def read_pair(ref, at):
    return ref[at:at + 8, :].astype(F32) + ref[at + 8:at + 16, :].astype(F32)


def back_call(x_at, pieces, wgu, wd, before, both, size, last):
    first = before is None

    def kernel(at_ref, a_ref, b_ref, c_ref, d_ref, wgu_ref, wd_ref, both_ref, *refs):
        refs = list(refs)
        if not first:
            before_ref, before_inner_ref = refs.pop(0), refs.pop(0)
        if last:
            own_ref, gain_ref, own_inner_ref, out_ref, acc_ref, inner_ref = refs
        elif first:
            acc_ref, inner_ref, inv_ref, all_inv_ref = refs
        else:
            acc_ref, inner_ref = refs
        gain_part = jnp.zeros((1, 512), F32)
        for k, ref in zip((0, 2, 1, -1), (a_ref, b_ref, c_ref, d_ref)):
            rows = block_rows(at_ref, -k)
            mixed = tn(ref[:size, :], wd_ref[...])
            grad = tn(ref[size:3 * size, :], wgu_ref[...])
            inner = read_pair(ref, 3 * size)
            if not first:
                mixed = mixed + before_ref[rows, :512]
                grad = grad + before_ref[rows, 512:]
                inner = inner + before_inner_ref[:, rows]
            acc_ref[rows, :512] = mixed
            acc_ref[rows, 512:] = grad
            inner_ref[:, rows] = inner
            if first:
                all_inv_ref[:, rows] = read_pair(ref, 3 * size + 16)
            if last:
                gain_part = gain_part + jnp.sum(grad * both_ref[rows, :512].astype(F32), axis=0, keepdims=True)
        if first:
            inv_ref[...] = all_inv_ref[:, :128]
        if last:
            own_ref[...] = acc_ref[:512, :]
            own_inner_ref[...] = inner_ref[:, :512]
            out_ref[:512, :] = acc_ref[512:, :].astype(BF)
            gain_part = jnp.broadcast_to(gain_part, (8, 512))
            gain_ref[...] = gain_part
            write_extra(out_ref, 512, gain_part, inner_ref[:, 512:])

    args = list(pieces) + [wgu, wd, both] + ([] if first else list(before))
    acc, inner = sds((1024, 1024), F32), sds((8, 1024), F32)
    if last:
        outs = [sds((512, 1024), F32), sds((8, 512), F32), sds((8, 512), F32), sds((520, 1024), BF)]
        scratch = [pltpu.VMEM(acc.shape, F32), pltpu.VMEM(inner.shape, F32)]
        return call(kernel, outs, (x_at,), *args, scratch=scratch)
    if first:
        return call(kernel, [acc, inner, sds((8, 128), F32)], (x_at,), *args, scratch=[pltpu.VMEM((8, 1024), F32)])
    return call(kernel, [acc, inner], (x_at,), *args)


def turn_left(inner, lanes):
    return jnp.concatenate(
        [pltpu.roll(inner[:, 128 * i:128 * (i + 1)], 128 - lanes, 1) for i in range(4)], axis=1)


def upper_half(inner):
    return jnp.concatenate([inner[:, 256:], inner[:, 256:]], axis=1)


def fold_call(own, gain_part, inner, messages, turns, strips):
    rows = own.shape[0]
    count = len(messages)
    keep = sum(size for _, size in strips[0])

    def kernel(own_ref, gain_ref, inner_ref, *refs):
        received = refs[:count]
        keep_ref, gain_out_ref, inner_out_ref = refs[count:count + 3]
        outs = refs[count + 3:]
        gain_sum, inner_sum = gain_ref[...], inner_ref[...]
        for ref, turn in zip(received, turns):
            gain_more, inner_more = read_extra(ref, rows)
            gain_sum = gain_sum + gain_more
            inner_sum = inner_sum + (turn(inner_more) if turn else inner_more)
        gain_out_ref[...] = gain_sum
        inner_out_ref[...] = inner_sum
        for strip, out in zip(strips, (keep_ref,) + tuple(outs)):
            to = 0
            for at, size in strip:
                total = own_ref[at:at + size, :]
                for ref in received:
                    total = total + ref[at:at + size, :].astype(F32)
                out[to:to + size, :] = total.astype(out.dtype)
                to += size
        for ref in outs:
            write_extra(ref, keep, gain_sum, inner_sum)

    outs = [sds((keep, 1024), F32), sds((8, 512), F32), sds((8, 512), F32)]
    outs += [sds((keep + 8, 1024), BF)] * (len(strips) - 1)
    return call(kernel, outs, (), own, gain_part, inner, *messages)


def as_column(rows):
    hi, lo = split(rows)
    eighth = jnp.full((16, 128), 0.125, BF)
    return tn(jnp.concatenate([hi, lo], axis=0), eighth)[:32, :1]


def final_call(own, gain_part, inner, inv, message, tokens, cotangent, gain):
    def kernel(own_ref, part_ref, inner_ref, inv_ref, a_ref, tok_ref, cot_ref, gain_ref, out_ref, grad_ref, vec_ref):
        total = own_ref[...] + a_ref[:32, :].astype(F32)
        gain_more, inner_more = read_extra(a_ref, 32)
        gain_sum = part_ref[...] + gain_more
        inner_sum = inner_ref[:, :128] + inner_more[:, 128:256]
        vec_ref[...] = gain_sum[:1, :]
        x = tok_ref[...].astype(F32)
        out_ref[...] = (x + total[:, :512]).astype(BF)
        scale = as_column(inv_ref[...]) * (as_column(inner_sum) / D)
        grad_ref[...] = (cot_ref[...].astype(F32) + total[:, 512:] * gain_ref[...] - x * scale).astype(BF)

    outs = [sds((32, 512), BF), sds((32, 512), BF), sds((1, 512), F32)]
    return call(kernel, outs, (), own, gain_part, inner, inv, message, tokens, cotangent, gain, hbm_out=(0, 1, 2))


def assemble_call(depth_at, groups):
    counts = [sum(len(pieces) for _, pieces in arrived) for _, arrived in groups]

    def kernel(at_ref, *refs):
        gate_ref, up_ref, down_ref, tgate_ref, tup_ref = refs[sum(counts):]
        refs = list(refs[:sum(counts)])
        for chunks, arrived in groups:
            segments = []
            for at, size in chunks:
                segments += [(ref, at, size) for ref in (down_ref, tgate_ref, tup_ref)]
            for source, pieces in arrived:
                base = (at_ref[0] ^ source) * FS
                todo = list(segments)
                for piece in pieces:
                    ref, to = refs.pop(0), 0
                    while to < piece.shape[0]:
                        target, at, size = todo.pop(0)
                        take = min(size, piece.shape[0] - to)
                        target[pl.ds(pl.multiple_of(base + at, 16), take), :] = ref[to:to + take, :]
                        to += take
                        if take < size:
                            todo.insert(0, (target, at + take, size - take))

        def turn(i, carry):
            cut = pl.ds(pl.multiple_of(i * 128, 128), 128)
            gate_ref[:, cut] = tgate_ref[cut, :].T
            up_ref[:, cut] = tup_ref[cut, :].T
            return carry

        lax.fori_loop(0, 14, turn, 0)

    args = [piece for _, arrived in groups for _, pieces in arrived for piece in pieces]
    outs = [sds((512, 4 * FS), BF), sds((512, 4 * FS), BF), sds((4 * FS, 512), BF)]
    scratch = [pltpu.VMEM((4 * FS, 512), BF), pltpu.VMEM((4 * FS, 512), BF)]
    return call(kernel, outs, (depth_at,), *args, scratch=scratch, hbm_out=(0, 1, 2), limit=24)


def step(tokens, norm_gain, w_gate, w_up, w_down, cotangent):
    x_at = jnp.reshape(lax.axis_index("row") // 2, (1,)).astype(jnp.int32)
    depth_at = jnp.reshape(lax.axis_index("depth"), (1,)).astype(jnp.int32)
    gain = norm_gain[None, :]
    count = len(CHUNKS)

    both = pack_call(tokens, cotangent)
    both = join_call([both] + [send_zl(both, k) for k in (1, 2, 3)])
    near = [send_y(both, k) for k in (1, 2, 3)]
    weights = prepare_call(depth_at, w_gate, w_up, w_down)
    both = join_call([both] + near)
    both = join_call([both, send_core(both)])
    chunks = [(at, size, weights[2 * i], weights[2 * i + 1]) for i, (at, size) in enumerate(CHUNKS)]

    received = []

    def partials(n):
        _, size, wgu, wd = chunks[n]
        arrived = []
        for ks in [(2,), (1,), (-1,)] if n == 0 else [(2, 1, -1)]:
            parts = partial_call(x_at, ks, both, gain, wgu, wd, size, n == 0)
            arrived += [send_x(part, k) for k, part in zip(ks, parts)]
        received.append(arrived)

    halves = []

    def row_sum(n):
        _, size, wgu, wd = chunks[n]
        total, message = sum_call(x_at, both, gain, wgu, wd, received[n], size, n == 0)
        halves.append((total, send_zh(message)))

    pieces = []

    def middle(n, inv):
        _, size, _, _ = chunks[n]
        mine, inv = middle_call(*halves[n], inv, size)
        pieces.append([mine] + [send_x(mine, k) for k in (2, 1, -1)])
        return inv

    def weight_grad(ns):
        grad = weight_grad_call(
            x_at, [pieces[n] for n in ns], [CHUNKS[n][1] for n in ns], both, gain)
        arrived = [(0, [grad])]
        return [CHUNKS[n] for n in ns], arrived

    def spread(group, ks):
        for k in ks:
            group[1].append((k, [send_y(group[1][0][1][0], k)]))

    def back(n, before):
        _, size, wgu, wd = chunks[n]
        return back_call(x_at, pieces[n], wgu, wd, before, both, size, n == count - 1)

    partials(0)
    partials(1)
    row_sum(0)
    partials(2)
    row_sum(1)
    inv = middle(0, None)
    row_sum(2)
    middle(1, inv)
    groups = [weight_grad((0,))]
    spread(groups[0], (2, 1, 3))
    *before, own_inv = back(0, None)
    middle(2, inv)
    groups.append(weight_grad((1,)))
    spread(groups[1], (2, 1, 3))
    before = back(1, before)
    own, gain_part, inner, message = back(2, before)
    message = send_core(message)
    groups.append(weight_grad((2,)))
    strips = [[(128 * a + 32 * j, 32) for a in range(4)] for j in range(4)]
    own, gain_part, inner, *messages = fold_call(own, gain_part, inner, [message], [None], strips)
    messages = [send_zl(m, k) for k, m in zip((1, 2, 3), messages)]
    spread(groups[2], (2, 1, 3))
    turns = [lambda v, lanes=lanes: turn_left(v, lanes) for lanes in (32, 64, 96)]
    own, gain_part, inner, *messages = fold_call(
        own, gain_part, inner, messages, turns, [[(0, 64)], [(64, 64)]])
    message = send_y(messages[0], 2)
    out_gate, out_up, out_down = assemble_call(depth_at, groups)
    own, gain_part, inner, *messages = fold_call(
        own, gain_part, inner, [message], [upper_half], [[(0, 32)], [(32, 32)]])
    message = send_y(messages[0], 1)
    output, grad_tokens, gain_grad = final_call(own, gain_part, inner, own_inv, message, tokens, cotangent, gain)
    return output, grad_tokens, gain_grad[0], out_gate, out_up, out_down


def solution(mesh):
    in_specs = (
        P(("col", "depth"), "row"),
        P("row"),
        P("row", "col"),
        P("row", "col"),
        P("col", "row"),
        P(("col", "depth"), "row"),
    )
    out_specs = (
        P(("col", "depth"), "row"),
        P(("col", "depth"), "row"),
        P("row"),
        P("row", "col"),
        P("row", "col"),
        P("col", "row"),
    )
    function = jax.shard_map(step, mesh=mesh, in_specs=in_specs, out_specs=out_specs, check_vma=False)
    shapes = [((1024, D), BF), ((D,), F32), ((D, 32 * FS), BF), ((D, 32 * FS), BF), ((32 * FS, D), BF), ((1024, D), BF)]
    jax.eval_shape(function, *[sds(*shape) for shape in shapes])
    return function
```

```python
import jax
import jax.numpy as jnp
from jax import lax
from jax.experimental import pallas as pl
from jax.experimental.pallas import tpu as pltpu
from jax.sharding import PartitionSpec as P


D = 4096
EPS = 1e-05
FS = 448
CHUNKS = ((0, 128), (128, 160), (288, 160))


BF = jnp.bfloat16
F32 = jnp.float32


def perm_x(k):
    return [(r, ((r // 2 + k) % 4) * 2 + r % 2) for r in range(8)]


PERM_ZH = [(r, r ^ 1) for r in range(8)]


def perm_zl(k):
    return [(c, c ^ (2 * k)) for c in range(8)]


PERM_CORE = [(c, c ^ 1) for c in range(8)]


def perm_y(k):
    return [(d, d ^ k) for d in range(4)]


def send(v, axis, perm):
    return lax.ppermute(v, axis, perm)


def send_x(v, k):
    return send(v, "row", perm_x(k))


def send_zh(v):
    return send(v, "row", PERM_ZH)


def send_zl(v, k):
    return send(v, "col", perm_zl(k))


def send_core(v):
    return send(v, "col", PERM_CORE)


def send_y(v, k):
    return send(v, "depth", perm_y(k))


def nt(left, right):
    return lax.dot_general(left, right, (((1,), (1,)), ((), ())), preferred_element_type=F32)


def nn(left, right):
    return lax.dot_general(left, right, (((1,), (0,)), ((), ())), preferred_element_type=F32)


def tn(left, right):
    return lax.dot_general(left, right, (((0,), (0,)), ((), ())), preferred_element_type=F32)


VM = pl.BlockSpec(memory_space=pltpu.VMEM)
SM = pl.BlockSpec(memory_space=pltpu.SMEM)


def sds(shape, dtype):
    return jax.ShapeDtypeStruct(shape, dtype)


ANY = pl.BlockSpec(memory_space=pl.ANY)


def call(kernel, outs, scalars, *args, scratch=(), raw=0, hbm_in=(), hbm_out=(), limit=12):
    outs = [o if i in hbm_out else pltpu.VMEM(o.shape, o.dtype) for i, o in enumerate(outs)]
    run = pl.pallas_call(
        kernel,
        out_shape=outs,
        in_specs=[SM] * len(scalars) + [ANY] * raw + [VM] * (len(args) - raw),
        out_specs=[VM] * len(outs),
        scratch_shapes=list(scratch),
        compiler_params=pltpu.CompilerParams(vmem_limit_bytes=limit << 20),
    )
    placed = [
        pltpu.with_memory_space_constraint(a, pltpu.HBM if i < raw or i in hbm_in else pltpu.VMEM)
        for i, a in enumerate(args)
    ]
    return run(*scalars, *placed)


def split(value):
    hi = value.astype(BF)
    return hi, (value - hi.astype(F32)).astype(BF)


def add_stat(message, size):
    return message[3 * size:3 * size + 8, :].astype(F32) + message[3 * size + 8:, :].astype(F32)


def pack_call(tokens, cotangent):
    def kernel(tok_ref, cot_ref, out_ref):
        out_ref[:, :512] = tok_ref[...]
        out_ref[:, 512:] = cot_ref[...]

    return call(kernel, [sds((32, 1024), BF)], (), tokens, cotangent, hbm_in=(0, 1))[0]


def join_call(parts):
    rows = parts[0].shape[0]

    def kernel(*refs):
        for i, ref in enumerate(refs[:-1]):
            refs[-1][rows * i:rows * (i + 1), :] = ref[...]

    return call(kernel, [sds((rows * len(parts), 1024), BF)], (), *parts)[0]


def prepare_call(depth_at, w_gate, w_up, w_down):
    def kernel(at_ref, gate_ref, up_ref, down_ref, *refs):
        outs, (cut_ref, turned_ref, sems) = refs[:-3], refs[-3:]
        at = at_ref[0]
        start = pl.multiple_of(((7 * at) // 2) * 128, 128)
        skip = pl.multiple_of((at % 2) * 64, 64)
        copies = [
            pltpu.make_async_copy(ref.at[:, pl.ds(start, 512)], cut_ref.at[i], sems.at[i])
            for i, ref in enumerate((gate_ref, up_ref))
        ]
        for i, (where, size) in enumerate(CHUNKS):
            rows = pl.ds(pl.multiple_of(at * FS + where, 16), size)
            copies.append(pltpu.make_async_copy(down_ref.at[rows, :], outs[2 * i + 1], sems.at[2 + i]))
        for copy in copies:
            copy.start()
        for which in (0, 1):
            copies[which].wait()
            turned_ref[which] = cut_ref[which].T
            for i, (where, size) in enumerate(CHUNKS):
                outs[2 * i][which * size:(which + 1) * size, :] = turned_ref[which, pl.ds(skip + where, size), :]
        for copy in copies[2:]:
            copy.wait()

    outs = []
    for _, size in CHUNKS:
        outs += [sds((2 * size, 512), BF), sds((size, 512), BF)]
    scratch = [pltpu.VMEM((2, 512, 512), BF), pltpu.VMEM((2, 512, 512), BF), pltpu.SemaphoreType.DMA((2 + len(CHUNKS),))]
    return call(kernel, outs, (depth_at,), w_gate, w_up, w_down, scratch=scratch, raw=3)


def block_rows(at_ref, k):
    return pl.ds(pl.multiple_of(((at_ref[0] + k + 4) % 4) * 256, 256), 256)


def block_part(rows, both_ref, gain_ref, wgu_ref, wd_ref, first):
    x = both_ref[rows, :512].astype(F32)
    parts = [nt(wgu_ref[...], (x * gain_ref[...]).astype(BF)), nt(wd_ref[...], both_ref[rows, 512:])]
    if first:
        hi, lo = split(x * x)
        ones = jnp.ones((8, 512), BF)
        parts.append(nt(ones, hi) + nt(ones, lo))
    return parts


def write_parts(ref, parts, size):
    ref[:2 * size, :] = parts[0].astype(BF)
    ref[2 * size:3 * size, :] = parts[1].astype(BF)
    if len(parts) > 2:
        hi, lo = split(parts[2])
        ref[3 * size:, :] = jnp.concatenate([hi, lo], axis=0)


def read_parts(ref, size, first):
    parts = [ref[:2 * size, :].astype(F32), ref[2 * size:3 * size, :].astype(F32)]
    if first:
        parts.append(add_stat(ref, size))
    return parts


def message_shape(size, first):
    return sds((3 * size + (16 if first else 0), 256), BF)


def partial_call(x_at, ks, both, gain, wgu, wd, size, first):
    def kernel(at_ref, both_ref, gain_ref, wgu_ref, wd_ref, *outs):
        for k, out_ref in zip(ks, outs):
            write_parts(out_ref, block_part(block_rows(at_ref, k), both_ref, gain_ref, wgu_ref, wd_ref, first), size)

    return call(kernel, [message_shape(size, first)] * len(ks), (x_at,), both, gain, wgu, wd)


def sum_call(x_at, both, gain, wgu, wd, received, size, first):
    def kernel(at_ref, both_ref, gain_ref, wgu_ref, wd_ref, a_ref, b_ref, c_ref, total_ref, out_ref):
        total = block_part(block_rows(at_ref, 0), both_ref, gain_ref, wgu_ref, wd_ref, first)
        for ref in (a_ref, b_ref, c_ref):
            total = [a + b for a, b in zip(total, read_parts(ref, size, first))]
        total_ref[:2 * size, :] = total[0]
        total_ref[2 * size:3 * size, :] = total[1]
        if first:
            total_ref[3 * size:, :] = total[2]
        write_parts(out_ref, total, size)

    outs = [sds((3 * size + (8 if first else 0), 256), F32), message_shape(size, first)]
    return call(kernel, outs, (x_at,), both, gain, wgu, wd, *received)


def middle_call(total, other, inv, size):
    first = inv is None

    def kernel(total_ref, other_ref, *refs):
        if first:
            out_ref, inv_ref = refs
            stat = total_ref[3 * size:, :] + add_stat(other_ref, size)
            inv_ref[...] = lax.rsqrt(stat / D + EPS)
        else:
            inv_ref, out_ref = refs
        scale = inv_ref[0:1, :]
        gate = (total_ref[:size, :] + other_ref[:size, :].astype(F32)) * scale
        up = (total_ref[size:2 * size, :] + other_ref[size:2 * size, :].astype(F32)) * scale
        grad = (total_ref[2 * size:3 * size, :] + other_ref[2 * size:3 * size, :].astype(F32)) * scale
        sig = jax.nn.sigmoid(gate)
        act = gate * sig
        out_ref[:size, :] = (act * up).astype(BF)
        grad_gate = grad * up * sig * (1.0 + gate * (1.0 - sig))
        grad_up = grad * act
        out_ref[size:2 * size, :] = grad_gate.astype(BF)
        out_ref[2 * size:3 * size, :] = grad_up.astype(BF)
        inner = jnp.sum(grad_gate * gate + grad_up * up, axis=0, keepdims=True)
        hi, lo = split(jnp.broadcast_to(inner, (8, 256)))
        out_ref[3 * size:3 * size + 16, :] = jnp.concatenate([hi, lo], axis=0)
        if first:
            hi, lo = split(inv_ref[...])
            out_ref[3 * size + 16:, :] = jnp.concatenate([hi, lo], axis=0)

    out = sds((3 * size + (32 if first else 16), 256), BF)
    if first:
        return call(kernel, [out, sds((8, 256), F32)], (), total, other)
    return call(kernel, [out], (), total, other, inv)[0], inv


def weight_grad_call(x_at, groups, sizes, both, gain):
    def kernel(at_ref, *refs):
        both_ref, gain_ref, out_ref = refs[-3:]
        to = 0
        for i, size in enumerate(sizes):
            down = jnp.zeros((size, 512), F32)
            gate_up = jnp.zeros((2 * size, 512), F32)
            for k, ref in zip((0, 2, 1, -1), refs[4 * i:4 * i + 4]):
                rows = block_rows(at_ref, -k)
                u = (both_ref[rows, :512].astype(F32) * gain_ref[...]).astype(BF)
                down = down + nn(ref[:size, :], both_ref[rows, 512:])
                gate_up = gate_up + nn(ref[size:3 * size, :], u)
            out_ref[to:to + size, :] = down.astype(BF)
            out_ref[to + size:to + 3 * size, :] = gate_up.astype(BF)
            to += 3 * size

    pieces = [piece for group in groups for piece in group]
    return call(kernel, [sds((3 * sum(sizes), 512), BF)], (x_at,), *pieces, both, gain)[0]


def write_extra(ref, rows, gain_part, inner):
    upper = lax.broadcasted_iota(jnp.int32, (8, 512), 0) < 4
    hi, lo = split(jnp.where(upper, gain_part, inner))
    ref[rows:, :512] = hi
    ref[rows:, 512:] = lo


def read_extra(ref, rows):
    extra = ref[rows:, :].astype(F32)
    extra = extra[:, :512] + extra[:, 512:]
    return jnp.broadcast_to(extra[:1, :], (8, 512)), jnp.broadcast_to(extra[4:5, :], (8, 512))


def read_pair(ref, at):
    return ref[at:at + 8, :].astype(F32) + ref[at + 8:at + 16, :].astype(F32)


def back_call(x_at, pieces, wgu, wd, before, both, size, last):
    first = before is None

    def kernel(at_ref, a_ref, b_ref, c_ref, d_ref, wgu_ref, wd_ref, both_ref, *refs):
        refs = list(refs)
        if not first:
            before_ref, before_inner_ref = refs.pop(0), refs.pop(0)
        if last:
            own_ref, gain_ref, own_inner_ref, out_ref, acc_ref, inner_ref = refs
        elif first:
            acc_ref, inner_ref, inv_ref, all_inv_ref = refs
        else:
            acc_ref, inner_ref = refs
        gain_part = jnp.zeros((1, 512), F32)
        for k, ref in zip((0, 2, 1, -1), (a_ref, b_ref, c_ref, d_ref)):
            rows = block_rows(at_ref, -k)
            mixed = tn(ref[:size, :], wd_ref[...])
            grad = tn(ref[size:3 * size, :], wgu_ref[...])
            inner = read_pair(ref, 3 * size)
            if not first:
                mixed = mixed + before_ref[rows, :512]
                grad = grad + before_ref[rows, 512:]
                inner = inner + before_inner_ref[:, rows]
            acc_ref[rows, :512] = mixed
            acc_ref[rows, 512:] = grad
            inner_ref[:, rows] = inner
            if first:
                all_inv_ref[:, rows] = read_pair(ref, 3 * size + 16)
            if last:
                gain_part = gain_part + jnp.sum(grad * both_ref[rows, :512].astype(F32), axis=0, keepdims=True)
        if first:
            inv_ref[...] = all_inv_ref[:, :128]
        if last:
            own_ref[...] = acc_ref[:512, :]
            own_inner_ref[...] = inner_ref[:, :512]
            out_ref[:512, :] = acc_ref[512:, :].astype(BF)
            gain_part = jnp.broadcast_to(gain_part, (8, 512))
            gain_ref[...] = gain_part
            write_extra(out_ref, 512, gain_part, inner_ref[:, 512:])

    args = list(pieces) + [wgu, wd, both] + ([] if first else list(before))
    acc, inner = sds((1024, 1024), F32), sds((8, 1024), F32)
    if last:
        outs = [sds((512, 1024), F32), sds((8, 512), F32), sds((8, 512), F32), sds((520, 1024), BF)]
        scratch = [pltpu.VMEM(acc.shape, F32), pltpu.VMEM(inner.shape, F32)]
        return call(kernel, outs, (x_at,), *args, scratch=scratch)
    if first:
        return call(kernel, [acc, inner, sds((8, 128), F32)], (x_at,), *args, scratch=[pltpu.VMEM((8, 1024), F32)])
    return call(kernel, [acc, inner], (x_at,), *args)


def turn_left(inner, lanes):
    return jnp.concatenate(
        [pltpu.roll(inner[:, 128 * i:128 * (i + 1)], 128 - lanes, 1) for i in range(4)], axis=1)


def upper_half(inner):
    return jnp.concatenate([inner[:, 256:], inner[:, 256:]], axis=1)


def fold_call(own, gain_part, inner, messages, turns, strips):
    rows = own.shape[0]
    count = len(messages)
    keep = sum(size for _, size in strips[0])

    def kernel(own_ref, gain_ref, inner_ref, *refs):
        received = refs[:count]
        keep_ref, gain_out_ref, inner_out_ref = refs[count:count + 3]
        outs = refs[count + 3:]
        gain_sum, inner_sum = gain_ref[...], inner_ref[...]
        for ref, turn in zip(received, turns):
            gain_more, inner_more = read_extra(ref, rows)
            gain_sum = gain_sum + gain_more
            inner_sum = inner_sum + (turn(inner_more) if turn else inner_more)
        gain_out_ref[...] = gain_sum
        inner_out_ref[...] = inner_sum
        for strip, out in zip(strips, (keep_ref,) + tuple(outs)):
            to = 0
            for at, size in strip:
                total = own_ref[at:at + size, :]
                for ref in received:
                    total = total + ref[at:at + size, :].astype(F32)
                out[to:to + size, :] = total.astype(out.dtype)
                to += size
        for ref in outs:
            write_extra(ref, keep, gain_sum, inner_sum)

    outs = [sds((keep, 1024), F32), sds((8, 512), F32), sds((8, 512), F32)]
    outs += [sds((keep + 8, 1024), BF)] * (len(strips) - 1)
    return call(kernel, outs, (), own, gain_part, inner, *messages)


def as_column(rows):
    hi, lo = split(rows)
    eighth = jnp.full((16, 128), 0.125, BF)
    return tn(jnp.concatenate([hi, lo], axis=0), eighth)[:32, :1]


def final_call(own, gain_part, inner, inv, message, tokens, cotangent, gain):
    def kernel(own_ref, part_ref, inner_ref, inv_ref, a_ref, tok_ref, cot_ref, gain_ref, out_ref, grad_ref, vec_ref):
        total = own_ref[...] + a_ref[:32, :].astype(F32)
        gain_more, inner_more = read_extra(a_ref, 32)
        gain_sum = part_ref[...] + gain_more
        inner_sum = inner_ref[:, :128] + inner_more[:, 128:256]
        vec_ref[...] = gain_sum[:1, :]
        x = tok_ref[...].astype(F32)
        out_ref[...] = (x + total[:, :512]).astype(BF)
        scale = as_column(inv_ref[...]) * (as_column(inner_sum) / D)
        grad_ref[...] = (cot_ref[...].astype(F32) + total[:, 512:] * gain_ref[...] - x * scale).astype(BF)

    outs = [sds((32, 512), BF), sds((32, 512), BF), sds((1, 512), F32)]
    return call(kernel, outs, (), own, gain_part, inner, inv, message, tokens, cotangent, gain, hbm_out=(0, 1, 2))


def assemble_call(depth_at, groups):
    counts = [sum(len(pieces) for _, pieces in arrived) for _, arrived in groups]

    def kernel(at_ref, *refs):
        gate_ref, up_ref, down_ref, tgate_ref, tup_ref = refs[sum(counts):]
        refs = list(refs[:sum(counts)])
        for chunks, arrived in groups:
            segments = []
            for at, size in chunks:
                segments += [(ref, at, size) for ref in (down_ref, tgate_ref, tup_ref)]
            for source, pieces in arrived:
                base = (at_ref[0] ^ source) * FS
                todo = list(segments)
                for piece in pieces:
                    ref, to = refs.pop(0), 0
                    while to < piece.shape[0]:
                        target, at, size = todo.pop(0)
                        take = min(size, piece.shape[0] - to)
                        target[pl.ds(pl.multiple_of(base + at, 16), take), :] = ref[to:to + take, :]
                        to += take
                        if take < size:
                            todo.insert(0, (target, at + take, size - take))

        def turn(i, carry):
            cut = pl.ds(pl.multiple_of(i * 128, 128), 128)
            gate_ref[:, cut] = tgate_ref[cut, :].T
            up_ref[:, cut] = tup_ref[cut, :].T
            return carry

        lax.fori_loop(0, 14, turn, 0)

    args = [piece for _, arrived in groups for _, pieces in arrived for piece in pieces]
    outs = [sds((512, 4 * FS), BF), sds((512, 4 * FS), BF), sds((4 * FS, 512), BF)]
    scratch = [pltpu.VMEM((4 * FS, 512), BF), pltpu.VMEM((4 * FS, 512), BF)]
    return call(kernel, outs, (depth_at,), *args, scratch=scratch, hbm_out=(0, 1, 2), limit=24)


def step(tokens, norm_gain, w_gate, w_up, w_down, cotangent):
    x_at = jnp.reshape(lax.axis_index("row") // 2, (1,)).astype(jnp.int32)
    depth_at = jnp.reshape(lax.axis_index("depth"), (1,)).astype(jnp.int32)
    gain = norm_gain[None, :]
    count = len(CHUNKS)

    both = pack_call(tokens, cotangent)
    both = join_call([both] + [send_zl(both, k) for k in (1, 2, 3)])
    near = [send_y(both, k) for k in (1, 2, 3)]
    weights = prepare_call(depth_at, w_gate, w_up, w_down)
    both = join_call([both] + near)
    both = join_call([both, send_core(both)])
    chunks = [(at, size, weights[2 * i], weights[2 * i + 1]) for i, (at, size) in enumerate(CHUNKS)]

    received = []

    def partials(n):
        _, size, wgu, wd = chunks[n]
        arrived = []
        for ks in [(2,), (1,), (-1,)] if n == 0 else [(2, 1, -1)]:
            parts = partial_call(x_at, ks, both, gain, wgu, wd, size, n == 0)
            arrived += [send_x(part, k) for k, part in zip(ks, parts)]
        received.append(arrived)

    halves = []

    def row_sum(n):
        _, size, wgu, wd = chunks[n]
        total, message = sum_call(x_at, both, gain, wgu, wd, received[n], size, n == 0)
        halves.append((total, send_zh(message)))

    pieces = []

    def middle(n, inv):
        _, size, _, _ = chunks[n]
        mine, inv = middle_call(*halves[n], inv, size)
        pieces.append([mine] + [send_x(mine, k) for k in (2, 1, -1)])
        return inv

    def weight_grad(ns):
        grad = weight_grad_call(
            x_at, [pieces[n] for n in ns], [CHUNKS[n][1] for n in ns], both, gain)
        arrived = [(0, [grad])]
        return [CHUNKS[n] for n in ns], arrived

    def spread(group, ks):
        for k in ks:
            group[1].append((k, [send_y(group[1][0][1][0], k)]))

    def relay(group):
        near = {source: pieces[0] for source, pieces in group[1]}
        half = near[0].shape[0] // 2
        group[1].append((2, [send_y(near[1][:half], 3), send_y(near[3][half:], 1)]))

    def back(n, before):
        _, size, wgu, wd = chunks[n]
        return back_call(x_at, pieces[n], wgu, wd, before, both, size, n == count - 1)

    partials(0)
    partials(1)
    row_sum(0)
    partials(2)
    row_sum(1)
    inv = middle(0, None)
    row_sum(2)
    middle(1, inv)
    groups = [weight_grad((0,))]
    spread(groups[0], (2, 1, 3))
    *before, own_inv = back(0, None)
    middle(2, inv)
    groups.append(weight_grad((1,)))
    spread(groups[1], (1, 3))
    before = back(1, before)
    own, gain_part, inner, message = back(2, before)
    message = send_core(message)
    groups.append(weight_grad((2,)))
    strips = [[(128 * a + 32 * j, 32) for a in range(4)] for j in range(4)]
    own, gain_part, inner, *messages = fold_call(own, gain_part, inner, [message], [None], strips)
    messages = [send_zl(m, k) for k, m in zip((1, 2, 3), messages)]
    relay(groups[1])
    spread(groups[2], (2, 1, 3))
    turns = [lambda v, lanes=lanes: turn_left(v, lanes) for lanes in (32, 64, 96)]
    own, gain_part, inner, *messages = fold_call(
        own, gain_part, inner, messages, turns, [[(0, 64)], [(64, 64)]])
    message = send_y(messages[0], 2)
    own, gain_part, inner, *messages = fold_call(
        own, gain_part, inner, [message], [upper_half], [[(0, 32)], [(32, 32)]])
    message = send_y(messages[0], 1)
    out_gate, out_up, out_down = assemble_call(depth_at, groups)
    output, grad_tokens, gain_grad = final_call(own, gain_part, inner, own_inv, message, tokens, cotangent, gain)
    return output, grad_tokens, gain_grad[0], out_gate, out_up, out_down


def solution(mesh):
    in_specs = (
        P(("col", "depth"), "row"),
        P("row"),
        P("row", "col"),
        P("row", "col"),
        P("col", "row"),
        P(("col", "depth"), "row"),
    )
    out_specs = (
        P(("col", "depth"), "row"),
        P(("col", "depth"), "row"),
        P("row"),
        P("row", "col"),
        P("row", "col"),
        P("col", "row"),
    )
    function = jax.shard_map(step, mesh=mesh, in_specs=in_specs, out_specs=out_specs, check_vma=False)
    shapes = [((1024, D), BF), ((D,), F32), ((D, 32 * FS), BF), ((D, 32 * FS), BF), ((32 * FS, D), BF), ((1024, D), BF)]
    jax.eval_shape(function, *[sds(*shape) for shape in shapes])
    return function
```

```python
import jax
import jax.numpy as jnp
from jax import lax
from jax.experimental import pallas as pl
from jax.experimental.pallas import tpu as pltpu
from jax.sharding import PartitionSpec as P


D = 4096
EPS = 1e-05
FS = 448
CHUNKS = ((0, 128), (128, 192), (320, 128))


BF = jnp.bfloat16
F32 = jnp.float32


def perm_x(k):
    return [(r, ((r // 2 + k) % 4) * 2 + r % 2) for r in range(8)]


PERM_ZH = [(r, r ^ 1) for r in range(8)]


def perm_zl(k):
    return [(c, c ^ (2 * k)) for c in range(8)]


PERM_CORE = [(c, c ^ 1) for c in range(8)]


def perm_y(k):
    return [(d, d ^ k) for d in range(4)]


def send(v, axis, perm):
    return lax.ppermute(v, axis, perm)


def send_x(v, k):
    return send(v, "row", perm_x(k))


def send_zh(v):
    return send(v, "row", PERM_ZH)


def send_zl(v, k):
    return send(v, "col", perm_zl(k))


def send_core(v):
    return send(v, "col", PERM_CORE)


def send_y(v, k):
    return send(v, "depth", perm_y(k))


def nt(left, right):
    return lax.dot_general(left, right, (((1,), (1,)), ((), ())), preferred_element_type=F32)


def nn(left, right):
    return lax.dot_general(left, right, (((1,), (0,)), ((), ())), preferred_element_type=F32)


def tn(left, right):
    return lax.dot_general(left, right, (((0,), (0,)), ((), ())), preferred_element_type=F32)


VM = pl.BlockSpec(memory_space=pltpu.VMEM)
SM = pl.BlockSpec(memory_space=pltpu.SMEM)


def sds(shape, dtype):
    return jax.ShapeDtypeStruct(shape, dtype)


ANY = pl.BlockSpec(memory_space=pl.ANY)


def call(kernel, outs, scalars, *args, scratch=(), raw=0, hbm_in=(), hbm_out=(), limit=12):
    outs = [o if i in hbm_out else pltpu.VMEM(o.shape, o.dtype) for i, o in enumerate(outs)]
    run = pl.pallas_call(
        kernel,
        out_shape=outs,
        in_specs=[SM] * len(scalars) + [ANY] * raw + [VM] * (len(args) - raw),
        out_specs=[VM] * len(outs),
        scratch_shapes=list(scratch),
        compiler_params=pltpu.CompilerParams(vmem_limit_bytes=limit << 20),
    )
    placed = [
        pltpu.with_memory_space_constraint(a, pltpu.HBM if i < raw or i in hbm_in else pltpu.VMEM)
        for i, a in enumerate(args)
    ]
    return run(*scalars, *placed)


def split(value):
    hi = value.astype(BF)
    return hi, (value - hi.astype(F32)).astype(BF)


def add_stat(message, size):
    return message[3 * size:3 * size + 8, :].astype(F32) + message[3 * size + 8:, :].astype(F32)


def pack_call(tokens, cotangent):
    def kernel(tok_ref, cot_ref, out_ref):
        out_ref[:, :512] = tok_ref[...]
        out_ref[:, 512:] = cot_ref[...]

    return call(kernel, [sds((32, 1024), BF)], (), tokens, cotangent, hbm_in=(0, 1))[0]


def join_call(parts):
    rows = parts[0].shape[0]

    def kernel(*refs):
        for i, ref in enumerate(refs[:-1]):
            refs[-1][rows * i:rows * (i + 1), :] = ref[...]

    return call(kernel, [sds((rows * len(parts), 1024), BF)], (), *parts)[0]


def prepare_call(depth_at, w_gate, w_up, w_down):
    def kernel(at_ref, gate_ref, up_ref, down_ref, *refs):
        outs, (cut_ref, turned_ref, sems) = refs[:-3], refs[-3:]
        at = at_ref[0]
        start = pl.multiple_of(((7 * at) // 2) * 128, 128)
        skip = pl.multiple_of((at % 2) * 64, 64)
        copies = [
            pltpu.make_async_copy(ref.at[:, pl.ds(start, 512)], cut_ref.at[i], sems.at[i])
            for i, ref in enumerate((gate_ref, up_ref))
        ]
        for i, (where, size) in enumerate(CHUNKS):
            rows = pl.ds(pl.multiple_of(at * FS + where, 16), size)
            copies.append(pltpu.make_async_copy(down_ref.at[rows, :], outs[2 * i + 1], sems.at[2 + i]))
        for copy in copies:
            copy.start()
        for which in (0, 1):
            copies[which].wait()
            turned_ref[which] = cut_ref[which].T
            for i, (where, size) in enumerate(CHUNKS):
                outs[2 * i][which * size:(which + 1) * size, :] = turned_ref[which, pl.ds(skip + where, size), :]
        for copy in copies[2:]:
            copy.wait()

    outs = []
    for _, size in CHUNKS:
        outs += [sds((2 * size, 512), BF), sds((size, 512), BF)]
    scratch = [pltpu.VMEM((2, 512, 512), BF), pltpu.VMEM((2, 512, 512), BF), pltpu.SemaphoreType.DMA((2 + len(CHUNKS),))]
    return call(kernel, outs, (depth_at,), w_gate, w_up, w_down, scratch=scratch, raw=3)


def block_rows(at_ref, k):
    return pl.ds(pl.multiple_of(((at_ref[0] + k + 4) % 4) * 256, 256), 256)


def block_part(rows, both_ref, gain_ref, wgu_ref, wd_ref, first):
    x = both_ref[rows, :512].astype(F32)
    parts = [nt(wgu_ref[...], (x * gain_ref[...]).astype(BF)), nt(wd_ref[...], both_ref[rows, 512:])]
    if first:
        hi, lo = split(x * x)
        ones = jnp.ones((8, 512), BF)
        parts.append(nt(ones, hi) + nt(ones, lo))
    return parts


def write_parts(ref, parts, size):
    ref[:2 * size, :] = parts[0].astype(BF)
    ref[2 * size:3 * size, :] = parts[1].astype(BF)
    if len(parts) > 2:
        hi, lo = split(parts[2])
        ref[3 * size:, :] = jnp.concatenate([hi, lo], axis=0)


def read_parts(ref, size, first):
    parts = [ref[:2 * size, :].astype(F32), ref[2 * size:3 * size, :].astype(F32)]
    if first:
        parts.append(add_stat(ref, size))
    return parts


def message_shape(size, first):
    return sds((3 * size + (16 if first else 0), 256), BF)


def partial_call(x_at, ks, both, gain, wgu, wd, size, first):
    def kernel(at_ref, both_ref, gain_ref, wgu_ref, wd_ref, *outs):
        for k, out_ref in zip(ks, outs):
            write_parts(out_ref, block_part(block_rows(at_ref, k), both_ref, gain_ref, wgu_ref, wd_ref, first), size)

    return call(kernel, [message_shape(size, first)] * len(ks), (x_at,), both, gain, wgu, wd)


def sum_call(x_at, both, gain, wgu, wd, received, size, first):
    def kernel(at_ref, both_ref, gain_ref, wgu_ref, wd_ref, a_ref, b_ref, c_ref, total_ref, out_ref):
        total = block_part(block_rows(at_ref, 0), both_ref, gain_ref, wgu_ref, wd_ref, first)
        for ref in (a_ref, b_ref, c_ref):
            total = [a + b for a, b in zip(total, read_parts(ref, size, first))]
        total_ref[:2 * size, :] = total[0]
        total_ref[2 * size:3 * size, :] = total[1]
        if first:
            total_ref[3 * size:, :] = total[2]
        write_parts(out_ref, total, size)

    outs = [sds((3 * size + (8 if first else 0), 256), F32), message_shape(size, first)]
    return call(kernel, outs, (x_at,), both, gain, wgu, wd, *received)


def middle_call(total, other, inv, size):
    first = inv is None

    def kernel(total_ref, other_ref, *refs):
        if first:
            out_ref, inv_ref = refs
            stat = total_ref[3 * size:, :] + add_stat(other_ref, size)
            inv_ref[...] = lax.rsqrt(stat / D + EPS)
        else:
            inv_ref, out_ref = refs
        scale = inv_ref[0:1, :]
        gate = (total_ref[:size, :] + other_ref[:size, :].astype(F32)) * scale
        up = (total_ref[size:2 * size, :] + other_ref[size:2 * size, :].astype(F32)) * scale
        grad = (total_ref[2 * size:3 * size, :] + other_ref[2 * size:3 * size, :].astype(F32)) * scale
        sig = jax.nn.sigmoid(gate)
        act = gate * sig
        out_ref[:size, :] = (act * up).astype(BF)
        grad_gate = grad * up * sig * (1.0 + gate * (1.0 - sig))
        grad_up = grad * act
        out_ref[size:2 * size, :] = grad_gate.astype(BF)
        out_ref[2 * size:3 * size, :] = grad_up.astype(BF)
        inner = jnp.sum(grad_gate * gate + grad_up * up, axis=0, keepdims=True)
        hi, lo = split(jnp.broadcast_to(inner, (8, 256)))
        out_ref[3 * size:3 * size + 16, :] = jnp.concatenate([hi, lo], axis=0)
        if first:
            hi, lo = split(inv_ref[...])
            out_ref[3 * size + 16:, :] = jnp.concatenate([hi, lo], axis=0)

    out = sds((3 * size + (32 if first else 16), 256), BF)
    if first:
        return call(kernel, [out, sds((8, 256), F32)], (), total, other)
    return call(kernel, [out], (), total, other, inv)[0], inv


def weight_grad_call(x_at, groups, sizes, both, gain):
    def kernel(at_ref, *refs):
        both_ref, gain_ref, out_ref = refs[-3:]
        to = 0
        for i, size in enumerate(sizes):
            down = jnp.zeros((size, 512), F32)
            gate_up = jnp.zeros((2 * size, 512), F32)
            for k, ref in zip((0, 2, 1, -1), refs[4 * i:4 * i + 4]):
                rows = block_rows(at_ref, -k)
                u = (both_ref[rows, :512].astype(F32) * gain_ref[...]).astype(BF)
                down = down + nn(ref[:size, :], both_ref[rows, 512:])
                gate_up = gate_up + nn(ref[size:3 * size, :], u)
            out_ref[to:to + size, :] = down.astype(BF)
            out_ref[to + size:to + 3 * size, :] = gate_up.astype(BF)
            to += 3 * size

    pieces = [piece for group in groups for piece in group]
    return call(kernel, [sds((3 * sum(sizes), 512), BF)], (x_at,), *pieces, both, gain)[0]


def write_extra(ref, rows, gain_part, inner):
    upper = lax.broadcasted_iota(jnp.int32, (8, 512), 0) < 4
    hi, lo = split(jnp.where(upper, gain_part, inner))
    ref[rows:, :512] = hi
    ref[rows:, 512:] = lo


def read_extra(ref, rows):
    extra = ref[rows:, :].astype(F32)
    extra = extra[:, :512] + extra[:, 512:]
    return jnp.broadcast_to(extra[:1, :], (8, 512)), jnp.broadcast_to(extra[4:5, :], (8, 512))


def read_pair(ref, at):
    return ref[at:at + 8, :].astype(F32) + ref[at + 8:at + 16, :].astype(F32)


def back_call(x_at, pieces, wgu, wd, before, both, size, last):
    first = before is None

    def kernel(at_ref, a_ref, b_ref, c_ref, d_ref, wgu_ref, wd_ref, both_ref, *refs):
        refs = list(refs)
        if not first:
            before_ref, before_inner_ref = refs.pop(0), refs.pop(0)
        if last:
            own_ref, gain_ref, own_inner_ref, out_ref, acc_ref, inner_ref = refs
        elif first:
            acc_ref, inner_ref, inv_ref, all_inv_ref = refs
        else:
            acc_ref, inner_ref = refs
        gain_part = jnp.zeros((1, 512), F32)
        for k, ref in zip((0, 2, 1, -1), (a_ref, b_ref, c_ref, d_ref)):
            rows = block_rows(at_ref, -k)
            mixed = tn(ref[:size, :], wd_ref[...])
            grad = tn(ref[size:3 * size, :], wgu_ref[...])
            inner = read_pair(ref, 3 * size)
            if not first:
                mixed = mixed + before_ref[rows, :512]
                grad = grad + before_ref[rows, 512:]
                inner = inner + before_inner_ref[:, rows]
            acc_ref[rows, :512] = mixed
            acc_ref[rows, 512:] = grad
            inner_ref[:, rows] = inner
            if first:
                all_inv_ref[:, rows] = read_pair(ref, 3 * size + 16)
            if last:
                gain_part = gain_part + jnp.sum(grad * both_ref[rows, :512].astype(F32), axis=0, keepdims=True)
        if first:
            inv_ref[...] = all_inv_ref[:, :128]
        if last:
            own_ref[...] = acc_ref[:512, :]
            own_inner_ref[...] = inner_ref[:, :512]
            out_ref[:512, :] = acc_ref[512:, :].astype(BF)
            gain_part = jnp.broadcast_to(gain_part, (8, 512))
            gain_ref[...] = gain_part
            write_extra(out_ref, 512, gain_part, inner_ref[:, 512:])

    args = list(pieces) + [wgu, wd, both] + ([] if first else list(before))
    acc, inner = sds((1024, 1024), F32), sds((8, 1024), F32)
    if last:
        outs = [sds((512, 1024), F32), sds((8, 512), F32), sds((8, 512), F32), sds((520, 1024), BF)]
        scratch = [pltpu.VMEM(acc.shape, F32), pltpu.VMEM(inner.shape, F32)]
        return call(kernel, outs, (x_at,), *args, scratch=scratch)
    if first:
        return call(kernel, [acc, inner, sds((8, 128), F32)], (x_at,), *args, scratch=[pltpu.VMEM((8, 1024), F32)])
    return call(kernel, [acc, inner], (x_at,), *args)


def turn_left(inner, lanes):
    return jnp.concatenate(
        [pltpu.roll(inner[:, 128 * i:128 * (i + 1)], 128 - lanes, 1) for i in range(4)], axis=1)


def upper_half(inner):
    return jnp.concatenate([inner[:, 256:], inner[:, 256:]], axis=1)


def fold_call(own, gain_part, inner, messages, turns, strips):
    rows = own.shape[0]
    count = len(messages)
    keep = sum(size for _, size in strips[0])

    def kernel(own_ref, gain_ref, inner_ref, *refs):
        received = refs[:count]
        keep_ref, gain_out_ref, inner_out_ref = refs[count:count + 3]
        outs = refs[count + 3:]
        gain_sum, inner_sum = gain_ref[...], inner_ref[...]
        for ref, turn in zip(received, turns):
            gain_more, inner_more = read_extra(ref, rows)
            gain_sum = gain_sum + gain_more
            inner_sum = inner_sum + (turn(inner_more) if turn else inner_more)
        gain_out_ref[...] = gain_sum
        inner_out_ref[...] = inner_sum
        for strip, out in zip(strips, (keep_ref,) + tuple(outs)):
            to = 0
            for at, size in strip:
                total = own_ref[at:at + size, :]
                for ref in received:
                    total = total + ref[at:at + size, :].astype(F32)
                out[to:to + size, :] = total.astype(out.dtype)
                to += size
        for ref in outs:
            write_extra(ref, keep, gain_sum, inner_sum)

    outs = [sds((keep, 1024), F32), sds((8, 512), F32), sds((8, 512), F32)]
    outs += [sds((keep + 8, 1024), BF)] * (len(strips) - 1)
    return call(kernel, outs, (), own, gain_part, inner, *messages)


def as_column(rows):
    hi, lo = split(rows)
    eighth = jnp.full((16, 128), 0.125, BF)
    return tn(jnp.concatenate([hi, lo], axis=0), eighth)[:32, :1]


def final_call(own, gain_part, inner, inv, message, tokens, cotangent, gain):
    def kernel(own_ref, part_ref, inner_ref, inv_ref, a_ref, tok_ref, cot_ref, gain_ref, out_ref, grad_ref, vec_ref):
        total = own_ref[...] + a_ref[:32, :].astype(F32)
        gain_more, inner_more = read_extra(a_ref, 32)
        gain_sum = part_ref[...] + gain_more
        inner_sum = inner_ref[:, :128] + inner_more[:, 128:256]
        vec_ref[...] = gain_sum[:1, :]
        x = tok_ref[...].astype(F32)
        out_ref[...] = (x + total[:, :512]).astype(BF)
        scale = as_column(inv_ref[...]) * (as_column(inner_sum) / D)
        grad_ref[...] = (cot_ref[...].astype(F32) + total[:, 512:] * gain_ref[...] - x * scale).astype(BF)

    outs = [sds((32, 512), BF), sds((32, 512), BF), sds((1, 512), F32)]
    return call(kernel, outs, (), own, gain_part, inner, inv, message, tokens, cotangent, gain, hbm_out=(0, 1, 2))


def assemble_call(depth_at, groups):
    counts = [sum(len(pieces) for _, pieces in arrived) for _, arrived in groups]

    def kernel(at_ref, *refs):
        gate_ref, up_ref, down_ref, tgate_ref, tup_ref = refs[sum(counts):]
        refs = list(refs[:sum(counts)])
        for chunks, arrived in groups:
            segments = []
            for at, size in chunks:
                segments += [(ref, at, size) for ref in (down_ref, tgate_ref, tup_ref)]
            for source, pieces in arrived:
                base = (at_ref[0] ^ source) * FS
                todo = list(segments)
                for piece in pieces:
                    ref, to = refs.pop(0), 0
                    while to < piece.shape[0]:
                        target, at, size = todo.pop(0)
                        take = min(size, piece.shape[0] - to)
                        target[pl.ds(pl.multiple_of(base + at, 16), take), :] = ref[to:to + take, :]
                        to += take
                        if take < size:
                            todo.insert(0, (target, at + take, size - take))

        def turn(i, carry):
            cut = pl.ds(pl.multiple_of(i * 128, 128), 128)
            gate_ref[:, cut] = tgate_ref[cut, :].T
            up_ref[:, cut] = tup_ref[cut, :].T
            return carry

        lax.fori_loop(0, 14, turn, 0)

    args = [piece for _, arrived in groups for _, pieces in arrived for piece in pieces]
    outs = [sds((512, 4 * FS), BF), sds((512, 4 * FS), BF), sds((4 * FS, 512), BF)]
    scratch = [pltpu.VMEM((4 * FS, 512), BF), pltpu.VMEM((4 * FS, 512), BF)]
    return call(kernel, outs, (depth_at,), *args, scratch=scratch, hbm_out=(0, 1, 2), limit=24)


def step(tokens, norm_gain, w_gate, w_up, w_down, cotangent):
    x_at = jnp.reshape(lax.axis_index("row") // 2, (1,)).astype(jnp.int32)
    depth_at = jnp.reshape(lax.axis_index("depth"), (1,)).astype(jnp.int32)
    gain = norm_gain[None, :]
    count = len(CHUNKS)

    both = pack_call(tokens, cotangent)
    both = join_call([both] + [send_zl(both, k) for k in (1, 2, 3)])
    near = [send_y(both, k) for k in (1, 2, 3)]
    weights = prepare_call(depth_at, w_gate, w_up, w_down)
    both = join_call([both] + near)
    both = join_call([both, send_core(both)])
    chunks = [(at, size, weights[2 * i], weights[2 * i + 1]) for i, (at, size) in enumerate(CHUNKS)]

    received = []

    def partials(n):
        _, size, wgu, wd = chunks[n]
        arrived = []
        for ks in [(2,), (1,), (-1,)] if n == 0 else [(2, 1, -1)]:
            parts = partial_call(x_at, ks, both, gain, wgu, wd, size, n == 0)
            arrived += [send_x(part, k) for k, part in zip(ks, parts)]
        received.append(arrived)

    halves = []

    def row_sum(n):
        _, size, wgu, wd = chunks[n]
        total, message = sum_call(x_at, both, gain, wgu, wd, received[n], size, n == 0)
        halves.append((total, send_zh(message)))

    pieces = []

    def middle(n, inv):
        _, size, _, _ = chunks[n]
        mine, inv = middle_call(*halves[n], inv, size)
        pieces.append([mine] + [send_x(mine, k) for k in (2, 1, -1)])
        return inv

    def weight_grad(ns):
        grad = weight_grad_call(
            x_at, [pieces[n] for n in ns], [CHUNKS[n][1] for n in ns], both, gain)
        arrived = [(0, [grad])]
        return [CHUNKS[n] for n in ns], arrived

    def spread(group, ks):
        for k in ks:
            group[1].append((k, [send_y(group[1][0][1][0], k)]))

    def relay(group):
        near = {source: pieces[0] for source, pieces in group[1]}
        half = near[0].shape[0] // 2
        group[1].append((2, [send_y(near[1][:half], 3), send_y(near[3][half:], 1)]))

    def back(n, before):
        _, size, wgu, wd = chunks[n]
        return back_call(x_at, pieces[n], wgu, wd, before, both, size, n == count - 1)

    partials(0)
    partials(1)
    row_sum(0)
    partials(2)
    row_sum(1)
    inv = middle(0, None)
    row_sum(2)
    middle(1, inv)
    groups = [weight_grad((0,))]
    spread(groups[0], (2, 1, 3))
    *before, own_inv = back(0, None)
    middle(2, inv)
    groups.append(weight_grad((1,)))
    spread(groups[1], (1, 3))
    before = back(1, before)
    own, gain_part, inner, message = back(2, before)
    message = send_core(message)
    groups.append(weight_grad((2,)))
    spread(groups[2], (1, 3))
    strips = [[(128 * a + 32 * j, 32) for a in range(4)] for j in range(4)]
    own, gain_part, inner, *messages = fold_call(own, gain_part, inner, [message], [None], strips)
    messages = [send_zl(m, k) for k, m in zip((1, 2, 3), messages)]
    relay(groups[1])
    spread(groups[2], (2,))
    turns = [lambda v, lanes=lanes: turn_left(v, lanes) for lanes in (32, 64, 96)]
    own, gain_part, inner, *messages = fold_call(
        own, gain_part, inner, messages, turns, [[(0, 64)], [(64, 64)]])
    message = send_y(messages[0], 2)
    own, gain_part, inner, *messages = fold_call(
        own, gain_part, inner, [message], [upper_half], [[(0, 32)], [(32, 32)]])
    message = send_y(messages[0], 1)
    out_gate, out_up, out_down = assemble_call(depth_at, groups)
    output, grad_tokens, gain_grad = final_call(own, gain_part, inner, own_inv, message, tokens, cotangent, gain)
    return output, grad_tokens, gain_grad[0], out_gate, out_up, out_down


def solution(mesh):
    in_specs = (
        P(("col", "depth"), "row"),
        P("row"),
        P("row", "col"),
        P("row", "col"),
        P("col", "row"),
        P(("col", "depth"), "row"),
    )
    out_specs = (
        P(("col", "depth"), "row"),
        P(("col", "depth"), "row"),
        P("row"),
        P("row", "col"),
        P("row", "col"),
        P("col", "row"),
    )
    function = jax.shard_map(step, mesh=mesh, in_specs=in_specs, out_specs=out_specs, check_vma=False)
    shapes = [((1024, D), BF), ((D,), F32), ((D, 32 * FS), BF), ((D, 32 * FS), BF), ((32 * FS, D), BF), ((1024, D), BF)]
    jax.eval_shape(function, *[sds(*shape) for shape in shapes])
    return function
```
